512 devices in a mesh: tile: 64 (over z, x, core), blk: 8 (over y).
Axes of the slice: x: 4, y: 8, z: 8, core: 2. Of those that a mesh axis runs over, the one named last changes fastest.
Arguments:
- ensemble: float32 [8, 5, 64, 256, 128], P('blk', None, None, 'tile'), may hold values from -6 to 6
- obs_col: int32 [13312], P('tile'), may hold values from 0 to 255, as said below
- obs_row: int32 [13312], P('tile'), may hold values from 0 to 127
- obs_level: int32 [13312], P('tile'), may hold values from 0 to 7
- obs_field: int32 [13312], P('tile'), may hold values from 0 to 4
- obs_batch: int32 [13312], P('tile'), may hold values from 0 to 3
- obs_value: float32 [13312], P('tile'), may hold values from -8 to 8
- obs_error: float32 [13312], P('tile'), may hold values from 0.3 to 3
- band_reach: int32 [8], replicated, may hold values from 1 to 6
Outputs:
- analysis: float32 [8, 5, 64, 256, 128], P('blk', None, None, 'tile')
The draws below stay inside these ranges and needn't reach their ends.
Inputs may be any that keep to these rules, and one draw needn't show every extreme that they name: `obs_col`: observation i lies in the strip of the tile that holds it: columns (i // 208) * 4 to (i // 208) * 4 + 3.
All inputs are finite; a program needn't handle non-finite values.
Results may differ from the reference program's by a relative error of at most 0.0003.
Values sent between devices are 32-bit elements; how exact they have to be, the bound alone decides.
A program may use at most 64 MiB of HBM per device.

```python
import math
import jax
import jax.numpy as jnp
from jax import lax

M = 64
FIELDS = 5
CX = 4
NY = 128
OBS_DEV = 208
NBATCH = 4
LEVELS = 8
NX = 256
NOBS = 13312
N_TILE = 64


def draw_obs_col(key, part):
    owner = jnp.arange(NOBS, dtype=jnp.int32) // OBS_DEV
    offset = jax.random.randint(key, (NOBS,), 0, CX, dtype=jnp.int32)
    offset = offset.at[0].set(0).at[NOBS - 1].set(CX - 1)
    return (owner * CX + offset).astype(jnp.int32)


def plant(drawn, key, low, top_value):
    index_at = [jax.random.randint(jax.random.fold_in(key, axis), (), 0, length) for axis, length in enumerate(drawn.shape)]
    main_axis = drawn.shape.index(max(drawn.shape))
    next_to = index_at[:main_axis] + [(index_at[main_axis] + 1) % drawn.shape[main_axis]] + index_at[main_axis + 1:]
    return drawn.at[tuple(index_at)].set(low).at[tuple(next_to)].set(top_value)


def steps_of(key, extent, shards, smallest, top_value):
    loudness, own = 1.0, jax.random.fold_in(key, 6)
    for axis_at, shards_of in shards:
        heights = jnp.exp(jax.random.uniform(jax.random.fold_in(own, axis_at), (shards_of,), jnp.float32, smallest / len(shards), top_value / len(shards)))
        loudness = loudness * jnp.repeat(heights, extent[axis_at] // shards_of).reshape([-1 if axis == axis_at else 1 for axis in range(len(extent))])
    return loudness


def noise(stream_key, extent, scale, bound, shards=(), kind=jnp.bfloat16):
    values = scale * jax.random.normal(stream_key, extent, jnp.float32)
    if shards:
        values = values * steps_of(stream_key, extent, shards, -0.22, 0.18)
    return jnp.clip(values, -bound, bound).astype(kind)


def setup_inputs(seed: int = 0) -> dict:
    key_of = jax.random.split(jax.random.key(seed), 10)
    return {
        "ensemble": noise(key_of[0], (LEVELS, FIELDS, M, NX, NY), 1.0, 6.0, ((0, 8), (3, 64)), jnp.float32),
        "obs_col": draw_obs_col(jax.random.fold_in(key_of[9], 71), 0),
        "obs_row": plant(jax.random.randint(key_of[2], (NOBS,), 0, NY), jax.random.fold_in(key_of[2], 1), 0, NY - 1).astype(jnp.int32),
        "obs_level": plant(jax.random.randint(key_of[3], (NOBS,), 0, LEVELS), jax.random.fold_in(key_of[3], 1), 0, LEVELS - 1).astype(jnp.int32),
        "obs_field": plant(jax.random.randint(key_of[4], (NOBS,), 0, FIELDS), jax.random.fold_in(key_of[4], 1), 0, FIELDS - 1).astype(jnp.int32),
        "obs_batch": plant(jax.random.randint(key_of[5], (NOBS,), 0, NBATCH), jax.random.fold_in(key_of[5], 1), 0, NBATCH - 1).astype(jnp.int32),
        "obs_value": noise(key_of[6], (NOBS,), 1.5, 8.0, ((0, 64),), jnp.float32),
        "obs_error": jnp.clip(jnp.exp(math.log(3.0) - 2.3025851 * jax.random.uniform(key_of[7], (NOBS,), jnp.float32) ** steps_of(key_of[7], (NOBS,), ((0, 64),), -0.2, 0.2)), 0.3, 3.0),
        "band_reach": plant(jax.random.randint(key_of[8], (LEVELS,), 1, 7), jax.random.fold_in(key_of[8], 1), 1, 6).astype(jnp.int32),
    }


def horizontal(src_col, src_row, dst_col, dst_row, radius):
    col_gap = (src_col[:, None] - dst_col[None, :]).astype(jnp.float32)
    row_gap = (src_row[:, None] - dst_row[None, :]).astype(jnp.float32)
    closeness = 1.0 - (col_gap * col_gap + row_gap * row_gap) / jnp.float32(radius * radius)
    return jnp.square(jnp.maximum(closeness, 0.0))

def batch_stats(near_priors, near_values, plus_batch, batch_turn):
    members = near_priors.shape[0]
    average = lax.optimization_barrier(jnp.mean(near_priors, axis=0))
    deviation = near_priors - average
    valid = plus_batch > 0
    active = plus_batch == batch_turn + 1
    error_var = jnp.where(valid, near_values[1], jnp.float32(1.0))
    total = lax.optimization_barrier(jnp.sum(deviation * deviation, axis=0)) / (members - 1) + error_var
    shrink = 1.0 / (1.0 + jnp.sqrt(error_var / total))
    innovation = near_values[0] - average
    coefficient = jnp.where(active, 1.0 / (total * (members - 1)), jnp.float32(0.0))
    return (deviation, innovation, coefficient, shrink)

def gain_apply(deviation, innovation, coefficient, shrink, taper, members):
    average = lax.optimization_barrier(jnp.mean(members, axis=0))
    spread = members - average
    covariance = lax.dot_general(deviation, spread, (((0,), (0,)), ((), ())), precision=lax.Precision.HIGHEST, preferred_element_type=jnp.float32)
    gain = covariance * taper * coefficient[:, None]
    average = average + jnp.dot(innovation, gain, precision=lax.Precision.HIGHEST, preferred_element_type=jnp.float32)
    spread = spread - jnp.dot(deviation * shrink, gain, precision=lax.Precision.HIGHEST, preferred_element_type=jnp.float32)
    return average + spread

def update_state(state, stats, near_level, taper_flat, reach_here, first_level, fields):
    deviation, innovation, coefficient, shrink = stats

    def one_slab(inputs):
        slab, slab_index = inputs
        level = first_level + slab_index // fields
        reach_level = reach_here[slab_index // fields]
        vertical = jnp.maximum(0.0, 1.0 - jnp.abs(level - near_level).astype(jnp.float32) / (reach_level + 1).astype(jnp.float32))
        return gain_apply(deviation, innovation, coefficient * vertical, shrink, taper_flat, slab)
    return lax.map(one_slab, (state, jnp.arange(state.shape[0], dtype=jnp.int32)))

def update_obs(own_priors, stats, near_places, own_places, band_reach, radius):
    deviation, innovation, coefficient, shrink = stats
    taper_obs = horizontal(near_places[0], near_places[1], own_places[0], own_places[1], radius)
    own_level = own_places[2]
    level_count = band_reach.shape[0]
    match = own_level[None, :] == jnp.arange(level_count, dtype=jnp.int32)[:, None]
    reach_own = lax.optimization_barrier(jnp.sum(jnp.where(match, band_reach[:, None], 0), axis=0))
    vertical = jnp.maximum(0.0, 1.0 - jnp.abs(own_level[None, :] - near_places[2][:, None]).astype(jnp.float32) / (reach_own[None, :] + 1).astype(jnp.float32))
    return gain_apply(deviation, innovation, coefficient, shrink, taper_obs * vertical, own_priors)

def reference(ensemble, obs_col, obs_row, obs_level, obs_field, obs_batch, obs_value, obs_error, band_reach):
    picked = ensemble[obs_level, obs_field, :, obs_col, obs_row]
    priors = picked.T.reshape(M, N_TILE, OBS_DEV).transpose(1, 0, 2)
    places = jnp.stack([obs_col, obs_row, obs_level, obs_field, obs_batch + 1]).reshape(5, N_TILE, OBS_DEV).transpose(1, 0, 2)
    values = jnp.stack([obs_value, obs_error]).reshape(2, N_TILE, OBS_DEV).transpose(1, 0, 2)

    def neighbours(array):
        padded = jnp.pad(array, ((1, 1), (0, 0), (0, 0)))
        return jnp.concatenate([padded[:-2], padded[1:-1], padded[2:]], axis=2)
    near_places = neighbours(places)
    near_values = neighbours(values)
    state = ensemble.reshape(LEVELS * FIELDS, M, N_TILE, CX * NY).transpose(2, 0, 1, 3)
    cells = jnp.arange(CX * NY, dtype=jnp.int32)
    tiles = jnp.arange(N_TILE, dtype=jnp.int32)
    for batch_turn in range(NBATCH):
        near_priors = neighbours(priors)

        def per_tile(inputs):
            tile_state, tile_priors, tile_near, tile_places, tile_near_places, tile_values, tile_index = inputs
            cell_col = tile_index * CX + cells // NY
            cell_row = cells % NY
            stats = batch_stats(tile_near, tile_values, tile_near_places[4], batch_turn)
            taper_flat = horizontal(tile_near_places[0], tile_near_places[1], cell_col, cell_row, CX)
            tile_state = update_state(tile_state, stats, tile_near_places[2], taper_flat, band_reach, 0, FIELDS)
            tile_priors = update_obs(tile_priors, stats, tile_near_places, tile_places, band_reach, CX)
            return (tile_state, tile_priors)
        state, priors = lax.map(per_tile, (state, priors, near_priors, places, near_places, near_values, tiles))
    return state.transpose(1, 2, 0, 3).reshape(LEVELS, FIELDS, M, NX, NY)
```

```python
import functools

import jax
import jax.numpy as jnp
from jax import lax
from jax.experimental import pallas as pl
from jax.experimental.pallas import tpu as pltpu
from jax.sharding import PartitionSpec as P

MESH = pl.DeviceIdType.MESH
NBATCH = 4
F32 = jnp.float32
BF16 = jnp.bfloat16
LANES = 128


def split(x):
    high = x.astype(BF16)
    low = (x - high.astype(F32)).astype(BF16)
    return high, low


def dot(a, b):
    return jnp.dot(a, b, preferred_element_type=F32)


def kernel(
    sizes,
    x_hbm,
    col_ref,
    row_ref,
    level_ref,
    field_ref,
    batch_ref,
    value_ref,
    error_ref,
    reach_ref,
    out_ref,
    x_in,
    state,
    near,
    meta,
    taper_state,
    taper_obs,
    picked,
    parts,
    dev_t,
    factor,
    load_sem,
    meta_send,
    meta_recv,
    rs_send,
    rs_recv,
    ag_send,
    ag_recv,
    halo_send,
    halo_recv,
):
    tiles, blocks, fields, members, cols, rows, obs, wide = sizes
    cells = cols * rows
    share = members // blocks
    tile = lax.axis_index("tile")
    level = lax.axis_index("blk")
    has_left, has_right = tile > 0, tile < tiles - 1

    load = pltpu.make_async_copy(x_hbm, x_in, load_sem)
    load.start()

    barrier = pltpu.get_barrier_semaphore()
    for step in range(1, blocks):
        pl.semaphore_signal(
            barrier, inc=1, device_id={"blk": lax.rem(level + step, blocks)}, device_id_type=MESH
        )

    @pl.when(has_left)
    def _():
        pl.semaphore_signal(barrier, inc=1, device_id={"tile": tile - 1}, device_id_type=MESH)

    @pl.when(has_right)
    def _():
        pl.semaphore_signal(barrier, inc=1, device_id={"tile": tile + 1}, device_id_type=MESH)

    meta[1] = jnp.zeros((8, wide), F32)
    meta[1, 0:1, :obs] = col_ref[...].astype(F32)
    meta[1, 1:2, :obs] = row_ref[...].astype(F32)
    meta[1, 2:3, :obs] = level_ref[...].astype(F32)
    meta[1, 3:4, :obs] = field_ref[...].astype(F32)
    meta[1, 4:5, :obs] = (batch_ref[...] + 1).astype(F32)
    meta[1, 5:6, :obs] = value_ref[...]
    meta[1, 6:7, :obs] = error_ref[...]

    @pl.when(jnp.logical_not(has_left))
    def _():
        near[:, 0] = jnp.zeros((NBATCH, members, wide), F32)
        meta[0] = jnp.zeros((8, wide), F32)

    @pl.when(jnp.logical_not(has_right))
    def _():
        near[:, 2] = jnp.zeros((NBATCH, members, wide), F32)
        meta[2] = jnp.zeros((8, wide), F32)

    pl.semaphore_wait(
        barrier, (blocks - 1) + has_left.astype(jnp.int32) + has_right.astype(jnp.int32)
    )

    def strips(array, send, recv):
        right = pltpu.make_async_remote_copy(
            src_ref=array.at[1],
            dst_ref=array.at[0],
            send_sem=send.at[0],
            recv_sem=recv.at[0],
            device_id={"tile": jnp.minimum(tile + 1, tiles - 1)},
            device_id_type=MESH,
        )
        left = pltpu.make_async_remote_copy(
            src_ref=array.at[1],
            dst_ref=array.at[2],
            send_sem=send.at[1],
            recv_sem=recv.at[1],
            device_id={"tile": jnp.maximum(tile - 1, 0)},
            device_id_type=MESH,
        )
        return right, left

    def strips_start(array, send, recv):
        right, left = strips(array, send, recv)
        pl.when(has_right)(right.start)
        pl.when(has_left)(left.start)

    def strips_arrive(array, send, recv):
        right, left = strips(array, send, recv)
        pl.when(has_left)(right.wait_recv)
        pl.when(has_right)(left.wait_recv)

    def strips_sent(array, send, recv):
        right, left = strips(array, send, recv)
        pl.when(has_right)(right.wait_send)
        pl.when(has_left)(left.wait_send)

    strips_start(meta, meta_send, meta_recv)

    own_col, own_row, own_level, own_field = (meta[1, i : i + 1, :] for i in range(4))
    here = (own_level == level.astype(F32)) & (meta[1, 4:5, :] > 0)
    place = (own_field * cols + own_col - (tile * cols).astype(F32)) * rows + own_row
    place = jnp.where(here, place, -1.0)
    load.wait()
    cell_at = lax.broadcasted_iota(jnp.int32, (cells, wide), 0).astype(F32)

    def slab(ref, f):
        return jnp.concatenate(
            [ref[pl.ds(f * members * cols + c, members, stride=cols), :] for c in range(cols)], axis=1
        )

    total = jnp.zeros((3 * members, wide), F32)
    for f in range(fields):
        x = slab(x_in, f)
        high = x.astype(BF16)
        rest = x - high.astype(F32)
        middle, low = split(rest)
        chosen = jnp.where(cell_at + float(f * cells) == place, 1.0, 0.0).astype(BF16)
        total = total + dot(jnp.concatenate([high, middle, low], axis=0), chosen)
    picked[...] = total[:members] + total[members : 2 * members] + total[2 * members :]

    def scatter(step):
        peer = lax.rem(level + step, blocks)
        return pltpu.make_async_remote_copy(
            src_ref=picked.at[pl.ds(pl.multiple_of(peer * share, share), share)],
            dst_ref=parts.at[step],
            send_sem=rs_send.at[step],
            recv_sem=rs_recv.at[step],
            device_id={"blk": peer},
            device_id_type=MESH,
        )

    mine = pl.ds(pl.multiple_of(level * share, share), share)

    def gather(step):
        peer = lax.rem(level + step, blocks)
        return pltpu.make_async_remote_copy(
            src_ref=near.at[0, 1, mine],
            dst_ref=near.at[0, 1, mine],
            send_sem=ag_send.at[step],
            recv_sem=ag_recv.at[step],
            device_id={"blk": peer},
            device_id_type=MESH,
        )

    def gather_arrive(step):
        source = lax.rem(level + blocks - step, blocks)
        at = pl.ds(pl.multiple_of(source * share, share), share)
        pltpu.make_async_remote_copy(
            src_ref=near.at[0, 1, at],
            dst_ref=near.at[0, 1, at],
            send_sem=ag_send.at[step],
            recv_sem=ag_recv.at[step],
            device_id={"blk": source},
            device_id_type=MESH,
        ).wait_recv()

    for step in range(1, blocks):
        scatter(step).start()

    strips_arrive(meta, meta_send, meta_recv)
    reach_here = reach_ref[level].astype(F32) + 1.0
    lane_row = lax.broadcasted_iota(jnp.int32, (obs, rows), 1).astype(F32)
    columns = []
    for s in range(3):
        turned = jnp.transpose(
            jnp.concatenate([meta[s], jnp.zeros((LANES - 8, wide), F32)], axis=0)
        )
        columns.append([turned[:obs, i : i + 1] for i in range(3)])
    for s in range(3):
        col, row, lev = columns[s]
        vertical = jnp.maximum(0.0, 1.0 - jnp.abs(level.astype(F32) - lev) / reach_here)
        gap = lane_row - row
        gap = gap * gap
        for c in range(cols):
            across = col - (tile * cols + c).astype(F32)
            close = jnp.maximum(1.0 - (across * across + gap) * (1.0 / (cols * cols)), 0.0)
            taper_state[s, :, c * rows : (c + 1) * rows] = close * close * vertical

    for step in range(1, blocks):
        scatter(step).wait_recv()
    summed = picked[mine, :]
    for step in range(1, blocks):
        summed = summed + parts[step]
    near[0, 1, mine, :] = summed
    for step in range(1, blocks):
        gather(step).start()

    reach_own = jnp.zeros((1, wide), F32)
    for k in range(blocks):
        reach_own = jnp.where(own_level == float(k), reach_ref[k].astype(F32), reach_own)
    reach_own = 1.0 / (reach_own + 1.0)
    for s in range(3):
        col, row, lev = columns[s]
        across = col - own_col
        gap = row - own_row
        close = jnp.maximum(1.0 - (across * across + gap * gap) * (1.0 / (cols * cols)), 0.0)
        vertical = jnp.maximum(0.0, 1.0 - jnp.abs(own_level - lev) * reach_own)
        taper_obs[s] = close * close * vertical

    for step in range(1, blocks):
        gather_arrive(step)
    strips_start(near.at[0], halo_send.at[0], halo_recv.at[0])

    first_half = lax.broadcasted_iota(jnp.int32, (wide, LANES), 1) < members

    def statistics(turn):
        for s in range(3):
            prior = near[turn, s]
            average = jnp.sum(prior, axis=0, keepdims=True) * (1.0 / members)
            deviation = prior - average
            flag = meta[s, 4:5, :]
            error = jnp.where(flag > 0, meta[s, 6:7, :], 1.0)
            spread = jnp.sum(deviation * deviation, axis=0, keepdims=True) * (1.0 / (members - 1)) + error
            shrink = 1.0 / (1.0 + jnp.sqrt(error / spread))
            innovation = meta[s, 5:6, :] - average
            coefficient = jnp.where(flag == float(turn + 1), 1.0 / (spread * (members - 1)), 0.0)
            weighted = deviation * coefficient
            turned = jnp.transpose(jnp.concatenate([weighted, weighted], axis=0))
            high = turned.astype(BF16).astype(F32)
            both = jnp.where(first_half, high, turned - high).astype(BF16)[:obs]
            dev_t[s] = jnp.concatenate([both, both], axis=1)
            high, low = split(innovation - shrink * deviation)
            factor[s] = jnp.concatenate([high, low], axis=0)

    def update(x, taper):
        high, low = split(x)
        stacked = jnp.concatenate([high, high, low, low], axis=0)
        for s in range(3):
            gain = dot(dev_t[s], stacked) * taper(s)
            gain_high, gain_low = split(gain)
            both = dot(factor[s, :, :obs], gain_high)
            x = x + (both[:members] + both[members:] + dot(factor[s, :members, :obs], gain_low))
        return x

    for turn in range(NBATCH):
        strips_arrive(near.at[turn], halo_send.at[turn], halo_recv.at[turn])
        statistics(turn)
        if turn + 1 < NBATCH:
            near[turn + 1, 1] = update(near[turn, 1], lambda s: taper_obs[s])
            strips_start(near.at[turn + 1], halo_send.at[turn + 1], halo_recv.at[turn + 1])

        def field(f, carry, turn=turn):
            for half in range(cells // wide):
                at = slice(half * wide, (half + 1) * wide)
                per = wide // rows
                if turn == 0:
                    x = jnp.concatenate(
                        [
                            x_in[pl.ds(f * members * cols + half * per + c, members, stride=cols), :]
                            for c in range(per)
                        ],
                        axis=1,
                    )
                else:
                    x = state[f, :, at]
                x = update(x, lambda s: taper_state[s, :, at])
                if turn + 1 < NBATCH:
                    state[f, :, at] = x
                else:
                    for c in range(per):
                        out_ref[pl.ds(f * members * cols + half * per + c, members, stride=cols), :] = x[
                            :, c * rows : (c + 1) * rows
                        ]
            return carry

        lax.fori_loop(0, fields, field, 0)

    strips_sent(meta, meta_send, meta_recv)
    for step in range(1, blocks):
        scatter(step).wait_send()
        gather(step).wait_send()
    for turn in range(NBATCH):
        strips_sent(near.at[turn], halo_send.at[turn], halo_recv.at[turn])


def shards(
    tiles, blocks, ensemble, obs_col, obs_row, obs_level, obs_field, obs_batch, obs_value, obs_error, band_reach
):
    levels, fields, members, cols, rows = ensemble.shape
    obs = obs_col.shape[0]
    wide = 256
    cells = cols * rows
    sizes = (tiles, blocks, fields, members, cols, rows, obs, wide)
    any_space = pl.BlockSpec(memory_space=pltpu.HBM)
    vmem = pl.BlockSpec(memory_space=pltpu.VMEM)
    smem = pl.BlockSpec(memory_space=pltpu.SMEM)
    flat = fields * members * cols
    out = pl.pallas_call(
        functools.partial(kernel, sizes),
        out_shape=jax.ShapeDtypeStruct((flat, rows), F32),
        in_specs=[any_space] + [vmem] * 7 + [smem],
        out_specs=vmem,
        scratch_shapes=[
            pltpu.VMEM((flat, rows), F32),
            pltpu.VMEM((fields, members, cells), F32),
            pltpu.VMEM((NBATCH, 3, members, wide), F32),
            pltpu.VMEM((3, 8, wide), F32),
            pltpu.VMEM((3, obs, cells), F32),
            pltpu.VMEM((3, obs, wide), F32),
            pltpu.VMEM((members, wide), F32),
            pltpu.VMEM((blocks, members // blocks, wide), F32),
            pltpu.VMEM((3, obs, wide), BF16),
            pltpu.VMEM((3, 2 * members, wide), BF16),
            pltpu.SemaphoreType.DMA,
            pltpu.SemaphoreType.DMA((2,)),
            pltpu.SemaphoreType.DMA((2,)),
            pltpu.SemaphoreType.DMA((blocks,)),
            pltpu.SemaphoreType.DMA((blocks,)),
            pltpu.SemaphoreType.DMA((blocks,)),
            pltpu.SemaphoreType.DMA((blocks,)),
            pltpu.SemaphoreType.DMA((NBATCH, 2)),
            pltpu.SemaphoreType.DMA((NBATCH, 2)),
        ],
        compiler_params=pltpu.CompilerParams(
            collective_id=0, has_side_effects=True, vmem_limit_bytes=32 * 2**20
        ),
    )(
        ensemble.reshape(flat, rows),
        *(v.reshape(1, obs) for v in (obs_col, obs_row, obs_level, obs_field, obs_batch, obs_value, obs_error)),
        band_reach,
    )
    return out.reshape(levels, fields, members, cols, rows)


def solution(mesh):
    return jax.shard_map(
        functools.partial(shards, mesh.shape["tile"], mesh.shape["blk"]),
        mesh=mesh,
        in_specs=(
            P("blk", None, None, "tile", None),
            P("tile"),
            P("tile"),
            P("tile"),
            P("tile"),
            P("tile"),
            P("tile"),
            P("tile"),
            P(),
        ),
        out_specs=P("blk", None, None, "tile", None),
        check_vma=False,
    )
```

```python
import functools

import jax
import jax.numpy as jnp
from jax import lax
from jax.experimental import pallas as pl
from jax.experimental.pallas import tpu as pltpu
from jax.sharding import PartitionSpec as P

MESH = pl.DeviceIdType.MESH
NBATCH = 4
F32 = jnp.float32
BF16 = jnp.bfloat16
LANES = 128
VMEM_LIMIT = 62


def split(x):
    high = x.astype(BF16)
    low = (x - high.astype(F32)).astype(BF16)
    return high, low


def dot(a, b):
    return jnp.dot(a, b, preferred_element_type=F32)


def kernel(
    sizes,
    x_hbm,
    col_ref,
    row_ref,
    level_ref,
    field_ref,
    batch_ref,
    value_ref,
    error_ref,
    reach_ref,
    out_ref,
    x_in,
    state,
    near,
    meta,
    taper_state,
    taper_obs,
    picked,
    parts,
    dev_t,
    factor,
    places,
    values,
    place_sem,
    load_sem,
    meta_send,
    meta_recv,
    rs_send,
    rs_recv,
    ag_send,
    ag_recv,
    halo_send,
    halo_recv,
):
    tiles, blocks, fields, members, cols, rows, obs, wide = sizes
    near_obs = dev_t.shape[0]
    cells = cols * rows
    share = members // blocks
    tile = lax.axis_index("tile")
    level = lax.axis_index("blk")
    has_left, has_right = tile > 0, tile < tiles - 1

    barrier = pltpu.get_barrier_semaphore()
    for step in range(1, blocks):
        pl.semaphore_signal(
            barrier, inc=1, device_id={"blk": lax.rem(level + step, blocks)}, device_id_type=MESH
        )

    @pl.when(has_left)
    def _():
        pl.semaphore_signal(barrier, inc=1, device_id={"tile": tile - 1}, device_id_type=MESH)

    @pl.when(has_right)
    def _():
        pl.semaphore_signal(barrier, inc=1, device_id={"tile": tile + 1}, device_id_type=MESH)

    brought = [
        pltpu.make_async_copy(ref, places.at[i], place_sem.at[i])
        for i, ref in enumerate((col_ref, row_ref, level_ref, field_ref, batch_ref))
    ] + [
        pltpu.make_async_copy(ref, values.at[i], place_sem.at[5 + i])
        for i, ref in enumerate((value_ref, error_ref))
    ]
    for copy in brought:
        copy.start()
    loads = [
        pltpu.make_async_copy(
            x_hbm.at[pl.ds(f * members * cols, members * cols)],
            x_in.at[pl.ds(f * members * cols, members * cols)],
            load_sem.at[f],
        )
        for f in range(fields)
    ]
    for copy in loads:
        copy.start()

    @pl.when(jnp.logical_not(has_left))
    def _():
        near[:, 0] = jnp.zeros((NBATCH, members, wide), F32)
        meta[0] = jnp.zeros((8, wide), F32)

    @pl.when(jnp.logical_not(has_right))
    def _():
        near[:, 2] = jnp.zeros((NBATCH, members, wide), F32)
        meta[2] = jnp.zeros((8, wide), F32)

    meta[1] = jnp.zeros((8, wide), F32)
    for copy in brought:
        copy.wait()
    for i in range(5):
        meta[1, i : i + 1, :obs] = (places[i] + (1 if i == 4 else 0)).astype(F32)
    for i in range(2):
        meta[1, 5 + i : 6 + i, :obs] = values[i]

    def strips(array, send, recv):
        right = pltpu.make_async_remote_copy(
            src_ref=array.at[1],
            dst_ref=array.at[0],
            send_sem=send.at[0],
            recv_sem=recv.at[0],
            device_id={"tile": jnp.minimum(tile + 1, tiles - 1)},
            device_id_type=MESH,
        )
        left = pltpu.make_async_remote_copy(
            src_ref=array.at[1],
            dst_ref=array.at[2],
            send_sem=send.at[1],
            recv_sem=recv.at[1],
            device_id={"tile": jnp.maximum(tile - 1, 0)},
            device_id_type=MESH,
        )
        return right, left

    def strips_start(array, send, recv):
        right, left = strips(array, send, recv)
        pl.when(has_right)(right.start)
        pl.when(has_left)(left.start)

    def strips_arrive(array, send, recv):
        right, left = strips(array, send, recv)
        pl.when(has_left)(right.wait_recv)
        pl.when(has_right)(left.wait_recv)

    def strips_sent(array, send, recv):
        right, left = strips(array, send, recv)
        pl.when(has_right)(right.wait_send)
        pl.when(has_left)(left.wait_send)

    own_col, own_row, own_level, own_field = (meta[1, i : i + 1, :] for i in range(4))
    here = (own_level == level.astype(F32)) & (meta[1, 4:5, :] > 0)
    place = (own_field * cols + own_col - (tile * cols).astype(F32)) * rows + own_row
    place = jnp.where(here, place, -1.0)
    cell_at = lax.broadcasted_iota(jnp.int32, (cells, wide), 0).astype(F32)

    def slab(ref, f):
        return jnp.concatenate(
            [ref[pl.ds(f * members * cols + c, members, stride=cols), :] for c in range(cols)], axis=1
        )

    total = jnp.zeros((3 * members, wide), F32)
    for f in range(fields):
        loads[f].wait()
        x = slab(x_in, f)
        high = x.astype(BF16)
        rest = x - high.astype(F32)
        middle, low = split(rest)
        chosen = jnp.where(cell_at + float(f * cells) == place, 1.0, 0.0).astype(BF16)
        total = total + dot(jnp.concatenate([high, middle, low], axis=0), chosen)
    picked[...] = total[:members] + total[members : 2 * members] + total[2 * members :]

    def scatter(step):
        peer = lax.rem(level + step, blocks)
        return pltpu.make_async_remote_copy(
            src_ref=picked.at[pl.ds(pl.multiple_of(peer * share, share), share)],
            dst_ref=parts.at[step],
            send_sem=rs_send.at[step],
            recv_sem=rs_recv.at[step],
            device_id={"blk": peer},
            device_id_type=MESH,
        )

    mine = pl.ds(pl.multiple_of(level * share, share), share)

    def gather(step):
        peer = lax.rem(level + step, blocks)
        return pltpu.make_async_remote_copy(
            src_ref=near.at[0, 1, mine],
            dst_ref=near.at[0, 1, mine],
            send_sem=ag_send.at[step],
            recv_sem=ag_recv.at[step],
            device_id={"blk": peer},
            device_id_type=MESH,
        )

    def gather_arrive(step):
        source = lax.rem(level + blocks - step, blocks)
        at = pl.ds(pl.multiple_of(source * share, share), share)
        pltpu.make_async_remote_copy(
            src_ref=near.at[0, 1, at],
            dst_ref=near.at[0, 1, at],
            send_sem=ag_send.at[step],
            recv_sem=ag_recv.at[step],
            device_id={"blk": source},
            device_id_type=MESH,
        ).wait_recv()

    pl.semaphore_wait(
        barrier, (blocks - 1) + has_left.astype(jnp.int32) + has_right.astype(jnp.int32)
    )
    for step in range(1, blocks):
        scatter(step).start()
    strips_start(meta, meta_send, meta_recv)

    strips_arrive(meta, meta_send, meta_recv)
    reach_here = reach_ref[level].astype(F32) + 1.0
    taper_state[3 * obs :] = jnp.zeros((near_obs - 3 * obs, cells), F32)
    taper_obs[3 * obs :] = jnp.zeros((near_obs - 3 * obs, wide), F32)
    dev_t[3 * obs :] = jnp.zeros((near_obs - 3 * obs, wide), BF16)
    lane_row = lax.broadcasted_iota(jnp.int32, (obs, rows), 1).astype(F32)
    columns = []
    for s in range(3):
        turned = jnp.transpose(
            jnp.concatenate([meta[s], jnp.zeros((LANES - 8, wide), F32)], axis=0)
        )
        columns.append([turned[:obs, i : i + 1] for i in range(3)])
    for s in range(3):
        col, row, lev = columns[s]
        vertical = jnp.maximum(0.0, 1.0 - jnp.abs(level.astype(F32) - lev) / reach_here)
        gap = lane_row - row
        gap = gap * gap
        for c in range(cols):
            across = col - (tile * cols + c).astype(F32)
            close = jnp.maximum(1.0 - (across * across + gap) * (1.0 / (cols * cols)), 0.0)
            taper_state[s * obs : (s + 1) * obs, c * rows : (c + 1) * rows] = close * close * vertical

    for step in range(1, blocks):
        scatter(step).wait_recv()
    summed = picked[mine, :]
    for step in range(1, blocks):
        summed = summed + parts[step]
    near[0, 1, mine, :] = summed
    for step in range(1, blocks):
        gather(step).start()

    reach_own = jnp.zeros((1, wide), F32)
    for k in range(blocks):
        reach_own = jnp.where(own_level == float(k), reach_ref[k].astype(F32), reach_own)
    reach_own = 1.0 / (reach_own + 1.0)
    for s in range(3):
        col, row, lev = columns[s]
        across = col - own_col
        gap = row - own_row
        close = jnp.maximum(1.0 - (across * across + gap * gap) * (1.0 / (cols * cols)), 0.0)
        vertical = jnp.maximum(0.0, 1.0 - jnp.abs(own_level - lev) * reach_own)
        taper_obs[s * obs : (s + 1) * obs] = close * close * vertical

    for step in range(1, blocks):
        gather_arrive(step)
    strips_start(near.at[0], halo_send.at[0], halo_recv.at[0])

    first_half = lax.broadcasted_iota(jnp.int32, (wide, LANES), 1) < members

    def statistics(turn):
        pulls = []
        for s in range(3):
            prior = near[turn, s]
            average = jnp.sum(prior, axis=0, keepdims=True) * (1.0 / members)
            deviation = prior - average
            flag = meta[s, 4:5, :]
            error = jnp.where(flag > 0, meta[s, 6:7, :], 1.0)
            spread = jnp.sum(deviation * deviation, axis=0, keepdims=True) * (1.0 / (members - 1)) + error
            shrink = 1.0 / (1.0 + jnp.sqrt(error / spread))
            innovation = meta[s, 5:6, :] - average
            coefficient = jnp.where(flag == float(turn + 1), 1.0 / (spread * (members - 1)), 0.0)
            weighted = deviation * coefficient
            turned = jnp.transpose(jnp.concatenate([weighted, weighted], axis=0))
            high = turned.astype(BF16).astype(F32)
            both = jnp.where(first_half, high, turned - high).astype(BF16)[:obs]
            dev_t[s * obs : (s + 1) * obs] = jnp.concatenate([both, both], axis=1)
            pulls.append((innovation - shrink * deviation)[:, :obs])
        pulls.append(jnp.zeros((members, near_obs - 3 * obs), F32))
        high, low = split(jnp.concatenate(pulls, axis=1))
        factor[...] = jnp.concatenate([high, low], axis=0)

    def update(x, taper):
        high, low = split(x)
        stacked = jnp.concatenate([high, high, low, low], axis=0)
        gain_high, gain_low = split(dot(dev_t[...], stacked) * taper())
        both = dot(factor[...], gain_high)
        x = x + (both[:members] + both[members:] + dot(factor[:members], gain_low))
        return x

    for turn in range(NBATCH):
        strips_arrive(near.at[turn], halo_send.at[turn], halo_recv.at[turn])
        statistics(turn)
        if turn + 1 < NBATCH:
            near[turn + 1, 1] = update(near[turn, 1], lambda: taper_obs[...])
            strips_start(near.at[turn + 1], halo_send.at[turn + 1], halo_recv.at[turn + 1])

        def field(f, carry, turn=turn):
            x = slab(x_in, f) if turn == 0 else state[f]
            x = update(x, lambda: taper_state[...])
            if turn + 1 < NBATCH:
                state[f] = x
            else:
                for c in range(cols):
                    out_ref[pl.ds(f * members * cols + c, members, stride=cols), :] = x[
                        :, c * rows : (c + 1) * rows
                    ]
            return carry

        lax.fori_loop(0, fields, field, 0)

    strips_sent(meta, meta_send, meta_recv)
    for step in range(1, blocks):
        scatter(step).wait_send()
        gather(step).wait_send()
    for turn in range(NBATCH):
        strips_sent(near.at[turn], halo_send.at[turn], halo_recv.at[turn])


def shards(
    tiles, blocks, ensemble, obs_col, obs_row, obs_level, obs_field, obs_batch, obs_value, obs_error, band_reach
):
    levels, fields, members, cols, rows = ensemble.shape
    obs = obs_col.shape[0]
    wide = 256
    cells = cols * rows
    sizes = (tiles, blocks, fields, members, cols, rows, obs, wide)
    any_space = pl.BlockSpec(memory_space=pltpu.HBM)
    vmem = pl.BlockSpec(memory_space=pltpu.VMEM)
    smem = pl.BlockSpec(memory_space=pltpu.SMEM)
    flat = fields * members * cols
    near_obs = -(-3 * obs // 32) * 32
    out = pl.pallas_call(
        functools.partial(kernel, sizes),
        out_shape=jax.ShapeDtypeStruct((flat, rows), F32),
        in_specs=[any_space] * 8 + [smem],
        out_specs=vmem,
        scratch_shapes=[
            pltpu.VMEM((flat, rows), F32),
            pltpu.VMEM((fields, members, cells), F32),
            pltpu.VMEM((NBATCH, 3, members, wide), F32),
            pltpu.VMEM((3, 8, wide), F32),
            pltpu.VMEM((near_obs, cells), F32),
            pltpu.VMEM((near_obs, wide), F32),
            pltpu.VMEM((members, wide), F32),
            pltpu.VMEM((blocks, members // blocks, wide), F32),
            pltpu.VMEM((near_obs, wide), BF16),
            pltpu.VMEM((2 * members, near_obs), BF16),
            pltpu.VMEM((5, 1, obs), jnp.int32),
            pltpu.VMEM((2, 1, obs), F32),
            pltpu.SemaphoreType.DMA((7,)),
            pltpu.SemaphoreType.DMA((fields,)),
            pltpu.SemaphoreType.DMA((2,)),
            pltpu.SemaphoreType.DMA((2,)),
            pltpu.SemaphoreType.DMA((blocks,)),
            pltpu.SemaphoreType.DMA((blocks,)),
            pltpu.SemaphoreType.DMA((blocks,)),
            pltpu.SemaphoreType.DMA((blocks,)),
            pltpu.SemaphoreType.DMA((NBATCH, 2)),
            pltpu.SemaphoreType.DMA((NBATCH, 2)),
        ],
        compiler_params=pltpu.CompilerParams(
            collective_id=0, has_side_effects=True, vmem_limit_bytes=VMEM_LIMIT * 2**20
        ),
    )(
        ensemble.reshape(flat, rows),
        *(v.reshape(1, obs) for v in (obs_col, obs_row, obs_level, obs_field, obs_batch, obs_value, obs_error)),
        band_reach,
    )
    return out.reshape(levels, fields, members, cols, rows)


def solution(mesh):
    return jax.shard_map(
        functools.partial(shards, mesh.shape["tile"], mesh.shape["blk"]),
        mesh=mesh,
        in_specs=(
            P("blk", None, None, "tile", None),
            P("tile"),
            P("tile"),
            P("tile"),
            P("tile"),
            P("tile"),
            P("tile"),
            P("tile"),
            P(),
        ),
        out_specs=P("blk", None, None, "tile", None),
        check_vma=False,
    )
```

```python
import functools

import jax
import jax.numpy as jnp
from jax import lax
from jax.experimental import pallas as pl
from jax.experimental.pallas import tpu as pltpu
from jax.sharding import PartitionSpec as P

MESH = pl.DeviceIdType.MESH
NBATCH = 4
F32 = jnp.float32
BF16 = jnp.bfloat16
LANES = 128
VMEM_LIMIT = 24


def split(x):
    high = x.astype(BF16)
    low = (x - high.astype(F32)).astype(BF16)
    return high, low


def dot(a, b):
    return jnp.dot(a, b, preferred_element_type=F32)


def update(x, dev_t, factor, taper):
    members = x.shape[0]
    high, low = split(x)
    stacked = jnp.concatenate([high, high, low, low], axis=0)
    gain_high, gain_low = split(dot(dev_t[...], stacked) * taper)
    both = dot(factor[...], gain_high)
    return x + (both[:members] + both[members:] + dot(factor[:members], gain_low))


def update_fields(xs, dev_t, factor, taper_state):
    taper = jnp.concatenate([taper_state[...]] * len(xs), axis=1)
    x = update(jnp.concatenate(xs, axis=1), dev_t, factor, taper)
    cells = x.shape[1] // len(xs)
    return [x[:, i * cells : (i + 1) * cells] for i in range(len(xs))]


def groups(fields):
    return [list(range(f, min(f + 2, fields))) for f in range(0, fields, 2)]


def finish(sizes, state, dev_t, factor, taper_state, out_hbm, out, out_sem):
    fields, members, cols, rows = sizes
    flat = members * cols
    copies = []
    for group in groups(fields):
        done = update_fields([state[f] for f in group], dev_t, factor, taper_state)
        for f, x in zip(group, done):
            for c in range(cols):
                out[pl.ds(f * flat + c, members, stride=cols), :] = x[:, c * rows : (c + 1) * rows]
            part = pl.ds(f * flat, flat)
            copies.append(pltpu.make_async_copy(out.at[part], out_hbm.at[part], out_sem.at[f]))
            copies[-1].start()
    for copy in copies:
        copy.wait()


def kernel(
    sizes,
    x_hbm,
    col_ref,
    row_ref,
    level_ref,
    field_ref,
    batch_ref,
    value_ref,
    error_ref,
    reach_hbm,
    state,
    dev_t,
    factor,
    taper_state,
    x_in,
    near,
    meta,
    taper_obs,
    picked,
    parts,
    places,
    values,
    reach_ref,
    reach_sem,
    place_sem,
    load_sem,
    meta_send,
    meta_recv,
    rs_send,
    rs_recv,
    ag_send,
    ag_recv,
    halo_send,
    halo_recv,
):
    tiles, blocks, fields, members, cols, rows, obs, wide = sizes
    near_obs = dev_t.shape[0]
    cells = cols * rows
    share = members // blocks
    tile = lax.axis_index("tile")
    level = lax.axis_index("blk")
    has_left, has_right = tile > 0, tile < tiles - 1

    barrier = pltpu.get_barrier_semaphore()
    for step in range(1, blocks):
        pl.semaphore_signal(
            barrier, inc=1, device_id={"blk": lax.rem(level + step, blocks)}, device_id_type=MESH
        )

    @pl.when(has_left)
    def _():
        pl.semaphore_signal(barrier, inc=1, device_id={"tile": tile - 1}, device_id_type=MESH)

    @pl.when(has_right)
    def _():
        pl.semaphore_signal(barrier, inc=1, device_id={"tile": tile + 1}, device_id_type=MESH)

    brought = [
        pltpu.make_async_copy(ref, places.at[i], place_sem.at[i])
        for i, ref in enumerate((col_ref, row_ref, level_ref, field_ref, batch_ref))
    ] + [
        pltpu.make_async_copy(ref, values.at[i], place_sem.at[5 + i])
        for i, ref in enumerate((value_ref, error_ref))
    ]
    reach_copy = pltpu.make_async_copy(reach_hbm, reach_ref, reach_sem)
    reach_copy.start()
    for copy in brought:
        copy.start()
    loads = [
        pltpu.make_async_copy(
            x_hbm.at[pl.ds(f * members * cols, members * cols)],
            x_in.at[pl.ds(f * members * cols, members * cols)],
            load_sem.at[f],
        )
        for f in range(fields)
    ]
    for copy in loads:
        copy.start()

    @pl.when(jnp.logical_not(has_left))
    def _():
        near[:, 0] = jnp.zeros((NBATCH, members, wide), F32)
        meta[0] = jnp.zeros((8, wide), F32)

    @pl.when(jnp.logical_not(has_right))
    def _():
        near[:, 2] = jnp.zeros((NBATCH, members, wide), F32)
        meta[2] = jnp.zeros((8, wide), F32)

    meta[1] = jnp.zeros((8, wide), F32)
    for copy in brought:
        copy.wait()
    for i in range(5):
        meta[1, i : i + 1, :obs] = (places[i] + (1 if i == 4 else 0)).astype(F32)
    for i in range(2):
        meta[1, 5 + i : 6 + i, :obs] = values[i]

    def strips(array, send, recv):
        right = pltpu.make_async_remote_copy(
            src_ref=array.at[1],
            dst_ref=array.at[0],
            send_sem=send.at[0],
            recv_sem=recv.at[0],
            device_id={"tile": jnp.minimum(tile + 1, tiles - 1)},
            device_id_type=MESH,
        )
        left = pltpu.make_async_remote_copy(
            src_ref=array.at[1],
            dst_ref=array.at[2],
            send_sem=send.at[1],
            recv_sem=recv.at[1],
            device_id={"tile": jnp.maximum(tile - 1, 0)},
            device_id_type=MESH,
        )
        return right, left

    def strips_start(array, send, recv):
        right, left = strips(array, send, recv)
        pl.when(has_right)(right.start)
        pl.when(has_left)(left.start)

    def strips_arrive(array, send, recv):
        right, left = strips(array, send, recv)
        pl.when(has_left)(right.wait_recv)
        pl.when(has_right)(left.wait_recv)

    def strips_sent(array, send, recv):
        right, left = strips(array, send, recv)
        pl.when(has_right)(right.wait_send)
        pl.when(has_left)(left.wait_send)

    own_col, own_row, own_level, own_field = (meta[1, i : i + 1, :] for i in range(4))
    here = (own_level == level.astype(F32)) & (meta[1, 4:5, :] > 0)
    place = (own_field * cols + own_col - (tile * cols).astype(F32)) * rows + own_row
    place = jnp.where(here, place, -1.0)
    cell_at = lax.broadcasted_iota(jnp.int32, (cells, wide), 0).astype(F32)

    def slab(ref, f):
        return jnp.concatenate(
            [ref[pl.ds(f * members * cols + c, members, stride=cols), :] for c in range(cols)], axis=1
        )

    total = jnp.zeros((3 * members, wide), F32)
    for f in range(fields):
        loads[f].wait()
        x = slab(x_in, f)
        high = x.astype(BF16)
        rest = x - high.astype(F32)
        middle, low = split(rest)
        chosen = jnp.where(cell_at + float(f * cells) == place, 1.0, 0.0).astype(BF16)
        total = total + dot(jnp.concatenate([high, middle, low], axis=0), chosen)
    picked[...] = total[:members] + total[members : 2 * members] + total[2 * members :]

    def scatter(step):
        peer = lax.rem(level + step, blocks)
        return pltpu.make_async_remote_copy(
            src_ref=picked.at[pl.ds(pl.multiple_of(peer * share, share), share)],
            dst_ref=parts.at[step],
            send_sem=rs_send.at[step],
            recv_sem=rs_recv.at[step],
            device_id={"blk": peer},
            device_id_type=MESH,
        )

    mine = pl.ds(pl.multiple_of(level * share, share), share)

    def gather(step):
        peer = lax.rem(level + step, blocks)
        return pltpu.make_async_remote_copy(
            src_ref=near.at[0, 1, mine],
            dst_ref=near.at[0, 1, mine],
            send_sem=ag_send.at[step],
            recv_sem=ag_recv.at[step],
            device_id={"blk": peer},
            device_id_type=MESH,
        )

    def gather_arrive(step):
        source = lax.rem(level + blocks - step, blocks)
        at = pl.ds(pl.multiple_of(source * share, share), share)
        pltpu.make_async_remote_copy(
            src_ref=near.at[0, 1, at],
            dst_ref=near.at[0, 1, at],
            send_sem=ag_send.at[step],
            recv_sem=ag_recv.at[step],
            device_id={"blk": source},
            device_id_type=MESH,
        ).wait_recv()

    pl.semaphore_wait(
        barrier, (blocks - 1) + has_left.astype(jnp.int32) + has_right.astype(jnp.int32)
    )
    for step in range(1, blocks):
        scatter(step).start()
    strips_start(meta, meta_send, meta_recv)

    strips_arrive(meta, meta_send, meta_recv)
    reach_copy.wait()
    reach_here = reach_ref[level].astype(F32) + 1.0
    taper_state[3 * obs :] = jnp.zeros((near_obs - 3 * obs, cells), F32)
    taper_obs[3 * obs :] = jnp.zeros((near_obs - 3 * obs, wide), F32)
    dev_t[3 * obs :] = jnp.zeros((near_obs - 3 * obs, wide), BF16)
    lane_row = lax.broadcasted_iota(jnp.int32, (obs, rows), 1).astype(F32)
    columns = []
    for s in range(3):
        turned = jnp.transpose(
            jnp.concatenate([meta[s], jnp.zeros((LANES - 8, wide), F32)], axis=0)
        )
        columns.append([turned[:obs, i : i + 1] for i in range(3)])
    for s in range(3):
        col, row, lev = columns[s]
        vertical = jnp.maximum(0.0, 1.0 - jnp.abs(level.astype(F32) - lev) / reach_here)
        gap = lane_row - row
        gap = gap * gap
        for c in range(cols):
            across = col - (tile * cols + c).astype(F32)
            close = jnp.maximum(1.0 - (across * across + gap) * (1.0 / (cols * cols)), 0.0)
            taper_state[s * obs : (s + 1) * obs, c * rows : (c + 1) * rows] = close * close * vertical

    for step in range(1, blocks):
        scatter(step).wait_recv()
    summed = picked[mine, :]
    for step in range(1, blocks):
        summed = summed + parts[step]
    near[0, 1, mine, :] = summed
    for step in range(1, blocks):
        gather(step).start()

    reach_own = jnp.zeros((1, wide), F32)
    for k in range(blocks):
        reach_own = jnp.where(own_level == float(k), reach_ref[k].astype(F32), reach_own)
    reach_own = 1.0 / (reach_own + 1.0)
    for s in range(3):
        col, row, lev = columns[s]
        across = col - own_col
        gap = row - own_row
        close = jnp.maximum(1.0 - (across * across + gap * gap) * (1.0 / (cols * cols)), 0.0)
        vertical = jnp.maximum(0.0, 1.0 - jnp.abs(own_level - lev) * reach_own)
        taper_obs[s * obs : (s + 1) * obs] = close * close * vertical

    for step in range(1, blocks):
        gather_arrive(step)
    strips_start(near.at[0], halo_send.at[0], halo_recv.at[0])

    first_half = lax.broadcasted_iota(jnp.int32, (wide, LANES), 1) < members

    def statistics(turn):
        pulls = []
        for s in range(3):
            prior = near[turn, s]
            average = jnp.sum(prior, axis=0, keepdims=True) * (1.0 / members)
            deviation = prior - average
            flag = meta[s, 4:5, :]
            error = jnp.where(flag > 0, meta[s, 6:7, :], 1.0)
            spread = jnp.sum(deviation * deviation, axis=0, keepdims=True) * (1.0 / (members - 1)) + error
            shrink = 1.0 / (1.0 + jnp.sqrt(error / spread))
            innovation = meta[s, 5:6, :] - average
            coefficient = jnp.where(flag == float(turn + 1), 1.0 / (spread * (members - 1)), 0.0)
            weighted = deviation * coefficient
            turned = jnp.transpose(jnp.concatenate([weighted, weighted], axis=0))
            high = turned.astype(BF16).astype(F32)
            both = jnp.where(first_half, high, turned - high).astype(BF16)[:obs]
            dev_t[s * obs : (s + 1) * obs] = jnp.concatenate([both, both], axis=1)
            pulls.append((innovation - shrink * deviation)[:, :obs])
        pulls.append(jnp.zeros((members, near_obs - 3 * obs), F32))
        high, low = split(jnp.concatenate(pulls, axis=1))
        factor[...] = jnp.concatenate([high, low], axis=0)

    for turn in range(NBATCH):
        strips_arrive(near.at[turn], halo_send.at[turn], halo_recv.at[turn])
        statistics(turn)
        if turn + 1 < NBATCH:
            near[turn + 1, 1] = update(near[turn, 1], dev_t, factor, taper_obs[...])
            strips_start(near.at[turn + 1], halo_send.at[turn + 1], halo_recv.at[turn + 1])
            for group in groups(fields):
                xs = [slab(x_in, f) if turn == 0 else state[f] for f in group]
                for f, x in zip(group, update_fields(xs, dev_t, factor, taper_state)):
                    state[f] = x

    strips_sent(meta, meta_send, meta_recv)
    for step in range(1, blocks):
        scatter(step).wait_send()
        gather(step).wait_send()
    for turn in range(NBATCH):
        strips_sent(near.at[turn], halo_send.at[turn], halo_recv.at[turn])


def shards(
    tiles, blocks, ensemble, obs_col, obs_row, obs_level, obs_field, obs_batch, obs_value, obs_error, band_reach
):
    levels, fields, members, cols, rows = ensemble.shape
    obs = obs_col.shape[0]
    wide = 256
    cells = cols * rows
    sizes = (tiles, blocks, fields, members, cols, rows, obs, wide)
    any_space = pl.BlockSpec(memory_space=pltpu.HBM)
    vmem = pl.BlockSpec(memory_space=pltpu.VMEM)
    in_hbm = functools.partial(pltpu.with_memory_space_constraint, memory_space=pltpu.HBM)
    flat = fields * members * cols
    near_obs = -(-3 * obs // 32) * 32
    made = pl.pallas_call(
        functools.partial(kernel, sizes),
        out_shape=(
            jax.ShapeDtypeStruct((fields, members, cells), F32),
            jax.ShapeDtypeStruct((near_obs, wide), BF16),
            jax.ShapeDtypeStruct((2 * members, near_obs), BF16),
            jax.ShapeDtypeStruct((near_obs, cells), F32),
        ),
        in_specs=[any_space] * 9,
        out_specs=[vmem] * 4,
        scratch_shapes=[
            pltpu.VMEM((flat, rows), F32),
            pltpu.VMEM((NBATCH, 3, members, wide), F32),
            pltpu.VMEM((3, 8, wide), F32),
            pltpu.VMEM((near_obs, wide), F32),
            pltpu.VMEM((members, wide), F32),
            pltpu.VMEM((blocks, members // blocks, wide), F32),
            pltpu.VMEM((5, 1, obs), jnp.int32),
            pltpu.VMEM((2, 1, obs), F32),
            pltpu.SMEM((blocks,), jnp.int32),
            pltpu.SemaphoreType.DMA,
            pltpu.SemaphoreType.DMA((7,)),
            pltpu.SemaphoreType.DMA((fields,)),
            pltpu.SemaphoreType.DMA((2,)),
            pltpu.SemaphoreType.DMA((2,)),
            pltpu.SemaphoreType.DMA((blocks,)),
            pltpu.SemaphoreType.DMA((blocks,)),
            pltpu.SemaphoreType.DMA((blocks,)),
            pltpu.SemaphoreType.DMA((blocks,)),
            pltpu.SemaphoreType.DMA((NBATCH, 2)),
            pltpu.SemaphoreType.DMA((NBATCH, 2)),
        ],
        compiler_params=pltpu.CompilerParams(
            collective_id=0, has_side_effects=True, vmem_limit_bytes=VMEM_LIMIT * 2**20
        ),
    )(
        in_hbm(ensemble.reshape(flat, rows)),
        *(
            in_hbm(v.reshape(1, obs))
            for v in (obs_col, obs_row, obs_level, obs_field, obs_batch, obs_value, obs_error)
        ),
        in_hbm(band_reach),
    )
    out = pl.pallas_call(
        functools.partial(finish, (fields, members, cols, rows)),
        out_shape=jax.ShapeDtypeStruct((flat, rows), F32),
        in_specs=[vmem] * 4,
        out_specs=any_space,
        scratch_shapes=[pltpu.VMEM((flat, rows), F32), pltpu.SemaphoreType.DMA((fields,))],
        compiler_params=pltpu.CompilerParams(vmem_limit_bytes=VMEM_LIMIT * 2**20),
    )(*made)
    return out.reshape(levels, fields, members, cols, rows)


def solution(mesh):
    return jax.shard_map(
        functools.partial(shards, mesh.shape["tile"], mesh.shape["blk"]),
        mesh=mesh,
        in_specs=(
            P("blk", None, None, "tile", None),
            P("tile"),
            P("tile"),
            P("tile"),
            P("tile"),
            P("tile"),
            P("tile"),
            P("tile"),
            P(),
        ),
        out_specs=P("blk", None, None, "tile", None),
        check_vma=False,
    )
```

```python
import functools

import jax
import jax.numpy as jnp
from jax import lax
from jax.experimental import pallas as pl
from jax.experimental.pallas import tpu as pltpu
from jax.sharding import PartitionSpec as P

MESH = pl.DeviceIdType.MESH
NBATCH = 4
F32 = jnp.float32
BF16 = jnp.bfloat16
LANES = 128
VMEM_LIMIT = 24
SHORT = 80


def split(x):
    high = x.astype(BF16)
    low = (x - high.astype(F32)).astype(BF16)
    return high, low


def sort_key(flag, axis):
    turn = jnp.where(flag > 0, NBATCH - flag, float(NBATCH))
    at = lax.broadcasted_iota(jnp.int32, flag.shape, axis).astype(F32)
    return turn * float(flag.shape[axis]) + at


def dot(a, b):
    return jnp.dot(a, b, preferred_element_type=F32)


def side_by_side(pulls, width):
    have = sum(pull.shape[1] for pull in pulls)
    pulls = pulls + [jnp.zeros((pulls[0].shape[0], width - have), F32)]
    high, low = split(jnp.concatenate(pulls, axis=1))
    return jnp.concatenate([high, low], axis=0)


def update(x, dev_t, factor, taper):
    members = x.shape[0]
    high, low = split(x)
    stacked = jnp.concatenate([high, high, low, low], axis=0)
    gain_high, gain_low = split(dot(dev_t[...], stacked) * taper)
    both = dot(factor[...], gain_high)
    return x + (both[:members] + both[members:] + dot(factor[:members], gain_low))


def update_fields(xs, dev_t, factor, taper):
    taper = jnp.concatenate([taper] * len(xs), axis=1)
    x = update(jnp.concatenate(xs, axis=1), dev_t, factor, taper)
    cells = x.shape[1] // len(xs)
    return [x[:, i * cells : (i + 1) * cells] for i in range(len(xs))]


def groups(fields):
    return [list(range(f, min(f + 2, fields))) for f in range(0, fields, 2)]


def finish(sizes, state, dev_t, factor, taper_state, short_factor, most, out_hbm, out, out_sem):
    fields, members, cols, rows, obs = sizes
    flat = members * cols

    def run(dev, pull, taper):
        copies = []
        for group in groups(fields):
            done = update_fields([state[f] for f in group], dev, pull, taper)
            for f, x in zip(group, done):
                for c in range(cols):
                    out[pl.ds(f * flat + c, members, stride=cols), :] = x[:, c * rows : (c + 1) * rows]
                part = pl.ds(f * flat, flat)
                copies.append(pltpu.make_async_copy(out.at[part], out_hbm.at[part], out_sem.at[f]))
                copies[-1].start()
        for copy in copies:
            copy.wait()

    few = jnp.max(most[...]) <= float(SHORT)

    @pl.when(few)
    def _():
        def starts(array):
            pieces = [array[s * obs : s * obs + SHORT] for s in range(3)]
            rest = short_factor.shape[1] - 3 * SHORT
            return jnp.concatenate(pieces + [jnp.zeros((rest, array.shape[1]), array.dtype)], axis=0)

        run(starts(dev_t), short_factor, starts(taper_state))

    @pl.when(jnp.logical_not(few))
    def _():
        run(dev_t, factor, taper_state[...])


def kernel(
    sizes,
    x_hbm,
    col_ref,
    row_ref,
    level_ref,
    field_ref,
    batch_ref,
    value_ref,
    error_ref,
    reach_hbm,
    state,
    dev_t,
    factor,
    taper_state,
    short_factor,
    most,
    x_in,
    near,
    meta,
    taper_obs,
    picked,
    parts,
    drawn,
    places,
    values,
    reach_ref,
    reach_sem,
    place_sem,
    load_sem,
    meta_send,
    meta_recv,
    rs_send,
    rs_recv,
    ag_send,
    ag_recv,
    halo_send,
    halo_recv,
    piece_send,
    piece_recv,
):
    tiles, blocks, fields, members, cols, rows, obs, wide = sizes
    near_obs = dev_t.shape[0]
    cells = cols * rows
    share = members // blocks
    tile = lax.axis_index("tile")
    level = lax.axis_index("blk")
    has_left, has_right = tile > 0, tile < tiles - 1

    barrier = pltpu.get_barrier_semaphore()
    for step in (4, 3, 5, 2, 6, 1, 7):
        pl.semaphore_signal(
            barrier, inc=1, device_id={"blk": lax.rem(level + step, blocks)}, device_id_type=MESH
        )

    @pl.when(has_left)
    def _():
        pl.semaphore_signal(barrier, inc=1, device_id={"tile": tile - 1}, device_id_type=MESH)

    @pl.when(has_right)
    def _():
        pl.semaphore_signal(barrier, inc=1, device_id={"tile": tile + 1}, device_id_type=MESH)

    brought = [
        pltpu.make_async_copy(ref, places.at[i], place_sem.at[i])
        for i, ref in enumerate((col_ref, row_ref, level_ref, field_ref, batch_ref))
    ] + [
        pltpu.make_async_copy(ref, values.at[i], place_sem.at[5 + i])
        for i, ref in enumerate((value_ref, error_ref))
    ]
    reach_copy = pltpu.make_async_copy(reach_hbm, reach_ref, reach_sem)
    reach_copy.start()
    for copy in brought:
        copy.start()
    loads = [
        pltpu.make_async_copy(
            x_hbm.at[pl.ds(f * members * cols, members * cols)],
            x_in.at[pl.ds(f * members * cols, members * cols)],
            load_sem.at[f],
        )
        for f in range(fields)
    ]
    for copy in loads:
        copy.start()

    @pl.when(jnp.logical_not(has_left))
    def _():
        near[:, 0] = jnp.zeros((NBATCH, members, wide), F32)
        meta[0] = jnp.zeros((8, wide), F32)

    @pl.when(jnp.logical_not(has_right))
    def _():
        near[:, 2] = jnp.zeros((NBATCH, members, wide), F32)
        meta[2] = jnp.zeros((8, wide), F32)

    drawn[...] = jnp.zeros_like(drawn)
    for copy in brought:
        copy.wait()
    for i in range(5):
        drawn[i : i + 1, :obs] = (places[i] + (1 if i == 4 else 0)).astype(F32)
    for i in range(2):
        drawn[5 + i : 6 + i, :obs] = values[i]
    unsorted = drawn[...]
    key = sort_key(unsorted[4:5], 1)
    turned = jnp.transpose(jnp.concatenate([unsorted, jnp.zeros((LANES - 8, wide), F32)], axis=0))
    key_column = sort_key(turned[:, 4:5], 0)
    rank = jnp.sum(jnp.where(key < key_column, 1.0, 0.0), axis=1, keepdims=True)
    moved = jnp.where(rank == lax.broadcasted_iota(jnp.int32, (wide, wide), 1).astype(F32), 1.0, 0.0)
    high = unsorted.astype(BF16).astype(F32)
    middle = (unsorted - high).astype(BF16).astype(F32)
    low = unsorted - high - middle
    terms = jnp.concatenate([high, middle, low, jnp.zeros_like(low)], axis=0).astype(BF16)
    terms = dot(terms, moved.astype(BF16))
    meta[1] = terms[:8] + terms[8:16] + terms[16:24]

    def strips(array, send, recv):
        right = pltpu.make_async_remote_copy(
            src_ref=array.at[1],
            dst_ref=array.at[0],
            send_sem=send.at[0],
            recv_sem=recv.at[0],
            device_id={"tile": jnp.minimum(tile + 1, tiles - 1)},
            device_id_type=MESH,
        )
        left = pltpu.make_async_remote_copy(
            src_ref=array.at[1],
            dst_ref=array.at[2],
            send_sem=send.at[1],
            recv_sem=recv.at[1],
            device_id={"tile": jnp.maximum(tile - 1, 0)},
            device_id_type=MESH,
        )
        return right, left

    def strips_start(array, send, recv):
        right, left = strips(array, send, recv)
        pl.when(has_right)(right.start)
        pl.when(has_left)(left.start)

    def strips_arrive(array, send, recv):
        right, left = strips(array, send, recv)
        pl.when(has_left)(right.wait_recv)
        pl.when(has_right)(left.wait_recv)

    def strips_sent(array, send, recv):
        right, left = strips(array, send, recv)
        pl.when(has_right)(right.wait_send)
        pl.when(has_left)(left.wait_send)

    own_col, own_row, own_level, own_field = (meta[1, i : i + 1, :] for i in range(4))
    here = (own_level == level.astype(F32)) & (meta[1, 4:5, :] > 0)
    place = (own_field * cols + own_col - (tile * cols).astype(F32)) * rows + own_row
    place = jnp.where(here, place, -1.0)
    cell_at = lax.broadcasted_iota(jnp.int32, (cells, wide), 0).astype(F32)

    def slab(ref, f):
        return jnp.concatenate(
            [ref[pl.ds(f * members * cols + c, members, stride=cols), :] for c in range(cols)], axis=1
        )

    total = jnp.zeros((3 * members, wide), F32)
    for f in range(fields):
        loads[f].wait()
        x = slab(x_in, f)
        high = x.astype(BF16)
        rest = x - high.astype(F32)
        middle, low = split(rest)
        chosen = jnp.where(cell_at + float(f * cells) == place, 1.0, 0.0).astype(BF16)
        total = total + dot(jnp.concatenate([high, middle, low], axis=0), chosen)
    picked[...] = total[:members] + total[members : 2 * members] + total[2 * members :]

    def scatter(step):
        peer = lax.rem(level + step, blocks)
        return pltpu.make_async_remote_copy(
            src_ref=picked.at[pl.ds(pl.multiple_of(peer * share, share), share)],
            dst_ref=parts.at[step],
            send_sem=rs_send.at[step],
            recv_sem=rs_recv.at[step],
            device_id={"blk": peer},
            device_id_type=MESH,
        )

    mine = pl.ds(pl.multiple_of(level * share, share), share)

    def gather(step):
        peer = lax.rem(level + step, blocks)
        return pltpu.make_async_remote_copy(
            src_ref=near.at[0, 1, mine],
            dst_ref=near.at[0, 1, mine],
            send_sem=ag_send.at[step],
            recv_sem=ag_recv.at[step],
            device_id={"blk": peer},
            device_id_type=MESH,
        )

    def gather_arrive(step):
        source = lax.rem(level + blocks - step, blocks)
        at = pl.ds(pl.multiple_of(source * share, share), share)
        pltpu.make_async_remote_copy(
            src_ref=near.at[0, 1, at],
            dst_ref=near.at[0, 1, at],
            send_sem=ag_send.at[step],
            recv_sem=ag_recv.at[step],
            device_id={"blk": source},
            device_id_type=MESH,
        ).wait_recv()

    pl.semaphore_wait(
        barrier, (blocks - 1) + has_left.astype(jnp.int32) + has_right.astype(jnp.int32)
    )
    for step in (4, 3, 5, 2, 6, 1, 7):
        scatter(step).start()
    strips_start(meta, meta_send, meta_recv)

    strips_arrive(meta, meta_send, meta_recv)
    reach_copy.wait()
    reach_here = reach_ref[level].astype(F32) + 1.0
    taper_state[3 * obs :] = jnp.zeros((near_obs - 3 * obs, cells), F32)
    taper_obs[3 * obs :] = jnp.zeros((near_obs - 3 * obs, wide), F32)
    dev_t[3 * obs :] = jnp.zeros((near_obs - 3 * obs, wide), BF16)
    lane_row = lax.broadcasted_iota(jnp.int32, (obs, rows), 1).astype(F32)
    columns = []
    for s in range(3):
        turned = jnp.transpose(
            jnp.concatenate([meta[s], jnp.zeros((LANES - 8, wide), F32)], axis=0)
        )
        columns.append([turned[:obs, i : i + 1] for i in range(3)])
    for s in range(3):
        col, row, lev = columns[s]
        vertical = jnp.maximum(0.0, 1.0 - jnp.abs(level.astype(F32) - lev) / reach_here)
        gap = lane_row - row
        gap = gap * gap
        for c in range(cols):
            across = col - (tile * cols + c).astype(F32)
            close = jnp.maximum(1.0 - (across * across + gap) * (1.0 / (cols * cols)), 0.0)
            taper_state[s * obs : (s + 1) * obs, c * rows : (c + 1) * rows] = close * close * vertical

    for step in range(1, blocks):
        scatter(step).wait_recv()
    summed = picked[mine, :]
    for step in range(1, blocks):
        summed = summed + parts[step]
    near[0, 1, mine, :] = summed
    for step in (4, 3, 5, 2, 6, 1, 7):
        gather(step).start()

    def pieces(source):
        at = pl.ds(pl.multiple_of(source * share, share), share)
        right = pltpu.make_async_remote_copy(
            src_ref=near.at[0, 1, at],
            dst_ref=near.at[0, 0, at],
            send_sem=piece_send.at[0, source],
            recv_sem=piece_recv.at[0, source],
            device_id={"tile": jnp.minimum(tile + 1, tiles - 1)},
            device_id_type=MESH,
        )
        left = pltpu.make_async_remote_copy(
            src_ref=near.at[0, 1, at],
            dst_ref=near.at[0, 2, at],
            send_sem=piece_send.at[1, source],
            recv_sem=piece_recv.at[1, source],
            device_id={"tile": jnp.maximum(tile - 1, 0)},
            device_id_type=MESH,
        )
        return right, left

    def piece_start(source):
        right, left = pieces(source)
        pl.when(has_right)(right.start)
        pl.when(has_left)(left.start)

    piece_start(level)

    reach_own = jnp.zeros((1, wide), F32)
    for k in range(blocks):
        reach_own = jnp.where(own_level == float(k), reach_ref[k].astype(F32), reach_own)
    reach_own = 1.0 / (reach_own + 1.0)
    for s in range(3):
        col, row, lev = columns[s]
        across = col - own_col
        gap = row - own_row
        close = jnp.maximum(1.0 - (across * across + gap * gap) * (1.0 / (cols * cols)), 0.0)
        vertical = jnp.maximum(0.0, 1.0 - jnp.abs(own_level - lev) * reach_own)
        taper_obs[s * obs : (s + 1) * obs] = close * close * vertical

    for step in (1, 7, 2, 6, 3, 5, 4):
        gather_arrive(step)
        piece_start(lax.rem(level + blocks - step, blocks))

    first_half = lax.broadcasted_iota(jnp.int32, (wide, LANES), 1) < members

    def statistics(turn):
        pulls = []
        for s in range(3):
            prior = near[turn, s]
            average = jnp.sum(prior, axis=0, keepdims=True) * (1.0 / members)
            deviation = prior - average
            flag = meta[s, 4:5, :]
            error = jnp.where(flag > 0, meta[s, 6:7, :], 1.0)
            spread = jnp.sum(deviation * deviation, axis=0, keepdims=True) * (1.0 / (members - 1)) + error
            shrink = 1.0 / (1.0 + jnp.sqrt(error / spread))
            innovation = meta[s, 5:6, :] - average
            coefficient = jnp.where(flag == float(turn + 1), 1.0 / (spread * (members - 1)), 0.0)
            weighted = deviation * coefficient
            turned = jnp.transpose(jnp.concatenate([weighted, weighted], axis=0))
            high = turned.astype(BF16).astype(F32)
            both = jnp.where(first_half, high, turned - high).astype(BF16)[:obs]
            dev_t[s * obs : (s + 1) * obs] = jnp.concatenate([both, both], axis=1)
            pulls.append((innovation - shrink * deviation)[:, :obs])
        factor[...] = side_by_side(pulls, near_obs)
        if turn + 1 == NBATCH:
            short_factor[...] = side_by_side([pull[:, :SHORT] for pull in pulls], wide)
            counts = [
                jnp.sum(jnp.where(meta[s, 4:5, :] == float(NBATCH), 1.0, 0.0), axis=1, keepdims=True)
                for s in range(3)
            ]
            most[...] = jnp.broadcast_to(functools.reduce(jnp.maximum, counts), (8, LANES))

    for turn in range(NBATCH):
        if turn:
            strips_arrive(near.at[turn], halo_send.at[turn], halo_recv.at[turn])
        else:
            for source in range(blocks):
                right, left = pieces(source)
                pl.when(has_left)(right.wait_recv)
                pl.when(has_right)(left.wait_recv)
        statistics(turn)
        if turn + 1 < NBATCH:
            near[turn + 1, 1] = update(near[turn, 1], dev_t, factor, taper_obs[...])
            strips_start(near.at[turn + 1], halo_send.at[turn + 1], halo_recv.at[turn + 1])
            for group in groups(fields):
                xs = [slab(x_in, f) if turn == 0 else state[f] for f in group]
                for f, x in zip(group, update_fields(xs, dev_t, factor, taper_state[...])):
                    state[f] = x

    strips_sent(meta, meta_send, meta_recv)
    for step in range(1, blocks):
        scatter(step).wait_send()
        gather(step).wait_send()
    for source in range(blocks):
        right, left = pieces(source)
        pl.when(has_right)(right.wait_send)
        pl.when(has_left)(left.wait_send)
    for turn in range(1, NBATCH):
        strips_sent(near.at[turn], halo_send.at[turn], halo_recv.at[turn])


def shards(
    tiles, blocks, ensemble, obs_col, obs_row, obs_level, obs_field, obs_batch, obs_value, obs_error, band_reach
):
    levels, fields, members, cols, rows = ensemble.shape
    obs = obs_col.shape[0]
    wide = 256
    cells = cols * rows
    sizes = (tiles, blocks, fields, members, cols, rows, obs, wide)
    any_space = pl.BlockSpec(memory_space=pltpu.HBM)
    vmem = pl.BlockSpec(memory_space=pltpu.VMEM)
    in_hbm = functools.partial(pltpu.with_memory_space_constraint, memory_space=pltpu.HBM)
    flat = fields * members * cols
    near_obs = -(-3 * obs // 32) * 32
    made = pl.pallas_call(
        functools.partial(kernel, sizes),
        out_shape=(
            jax.ShapeDtypeStruct((fields, members, cells), F32),
            jax.ShapeDtypeStruct((near_obs, wide), BF16),
            jax.ShapeDtypeStruct((2 * members, near_obs), BF16),
            jax.ShapeDtypeStruct((near_obs, cells), F32),
            jax.ShapeDtypeStruct((2 * members, wide), BF16),
            jax.ShapeDtypeStruct((8, LANES), F32),
        ),
        in_specs=[any_space] * 9,
        out_specs=[vmem] * 6,
        scratch_shapes=[
            pltpu.VMEM((flat, rows), F32),
            pltpu.VMEM((NBATCH, 3, members, wide), F32),
            pltpu.VMEM((3, 8, wide), F32),
            pltpu.VMEM((near_obs, wide), F32),
            pltpu.VMEM((members, wide), F32),
            pltpu.VMEM((blocks, members // blocks, wide), F32),
            pltpu.VMEM((8, wide), F32),
            pltpu.VMEM((5, 1, obs), jnp.int32),
            pltpu.VMEM((2, 1, obs), F32),
            pltpu.SMEM((blocks,), jnp.int32),
            pltpu.SemaphoreType.DMA,
            pltpu.SemaphoreType.DMA((7,)),
            pltpu.SemaphoreType.DMA((fields,)),
            pltpu.SemaphoreType.DMA((2,)),
            pltpu.SemaphoreType.DMA((2,)),
            pltpu.SemaphoreType.DMA((blocks,)),
            pltpu.SemaphoreType.DMA((blocks,)),
            pltpu.SemaphoreType.DMA((blocks,)),
            pltpu.SemaphoreType.DMA((blocks,)),
            pltpu.SemaphoreType.DMA((NBATCH, 2)),
            pltpu.SemaphoreType.DMA((NBATCH, 2)),
            pltpu.SemaphoreType.DMA((2, blocks)),
            pltpu.SemaphoreType.DMA((2, blocks)),
        ],
        compiler_params=pltpu.CompilerParams(
            collective_id=0, has_side_effects=True, vmem_limit_bytes=VMEM_LIMIT * 2**20
        ),
    )(
        in_hbm(ensemble.reshape(flat, rows)),
        *(
            in_hbm(v.reshape(1, obs))
            for v in (obs_col, obs_row, obs_level, obs_field, obs_batch, obs_value, obs_error)
        ),
        in_hbm(band_reach),
    )
    out = pl.pallas_call(
        functools.partial(finish, (fields, members, cols, rows, obs)),
        out_shape=jax.ShapeDtypeStruct((flat, rows), F32),
        in_specs=[vmem] * 6,
        out_specs=any_space,
        scratch_shapes=[pltpu.VMEM((flat, rows), F32), pltpu.SemaphoreType.DMA((fields,))],
        compiler_params=pltpu.CompilerParams(vmem_limit_bytes=VMEM_LIMIT * 2**20),
    )(*made)
    return out.reshape(levels, fields, members, cols, rows)


def solution(mesh):
    return jax.shard_map(
        functools.partial(shards, mesh.shape["tile"], mesh.shape["blk"]),
        mesh=mesh,
        in_specs=(
            P("blk", None, None, "tile", None),
            P("tile"),
            P("tile"),
            P("tile"),
            P("tile"),
            P("tile"),
            P("tile"),
            P("tile"),
            P(),
        ),
        out_specs=P("blk", None, None, "tile", None),
        check_vma=False,
    )
```

```python
import functools

import jax
import jax.numpy as jnp
from jax import lax
from jax.experimental import pallas as pl
from jax.experimental.pallas import tpu as pltpu
from jax.sharding import PartitionSpec as P

MESH = pl.DeviceIdType.MESH
NBATCH = 4
F32 = jnp.float32
BF16 = jnp.bfloat16
LANES = 128
VMEM_LIMIT = 24
SHORT = 80


def split(x):
    high = x.astype(BF16)
    low = (x - high.astype(F32)).astype(BF16)
    return high, low


def sort_key(flag, axis):
    turn = jnp.where(flag > 0, NBATCH - flag, float(NBATCH))
    at = lax.broadcasted_iota(jnp.int32, flag.shape, axis).astype(F32)
    return turn * float(flag.shape[axis]) + at


def dot(a, b):
    return jnp.dot(a, b, preferred_element_type=F32)


def side_by_side(pulls, width):
    have = sum(pull.shape[1] for pull in pulls)
    pulls = pulls + [jnp.zeros((pulls[0].shape[0], width - have), F32)]
    high, low = split(jnp.concatenate(pulls, axis=1))
    return jnp.concatenate([high, low], axis=0)


def update(x, dev_t, factor, taper):
    members = x.shape[0]
    high, low = split(x)
    stacked = jnp.concatenate([high, high, low, low], axis=0)
    gain_high, gain_low = split(dot(dev_t[...], stacked) * taper)
    both = dot(factor[...], gain_high)
    return x + (both[:members] + both[members:] + dot(factor[:members], gain_low))


def update_fields(xs, dev_t, factor, taper):
    taper = jnp.concatenate([taper] * len(xs), axis=1)
    x = update(jnp.concatenate(xs, axis=1), dev_t, factor, taper)
    cells = x.shape[1] // len(xs)
    return [x[:, i * cells : (i + 1) * cells] for i in range(len(xs))]


def groups(fields):
    return [list(range(f, min(f + 2, fields))) for f in range(0, fields, 2)]


def finish(sizes, state, dev_t, factor, taper_state, short_factor, most, out_hbm, out, out_sem):
    fields, members, cols, rows, obs = sizes
    flat = members * cols

    def run(dev, pull, taper):
        copies = []
        for group in [list(range(fields))]:
            done = update_fields([state[f] for f in group], dev, pull, taper)
            for f, x in zip(group, done):
                for c in range(cols):
                    out[pl.ds(f * flat + c, members, stride=cols), :] = x[:, c * rows : (c + 1) * rows]
                part = pl.ds(f * flat, flat)
                copies.append(pltpu.make_async_copy(out.at[part], out_hbm.at[part], out_sem.at[f]))
                copies[-1].start()
        for copy in copies:
            copy.wait()

    few = jnp.max(most[...]) <= float(SHORT)

    @pl.when(few)
    def _():
        def starts(array):
            pieces = [array[s * obs : s * obs + SHORT] for s in range(3)]
            rest = short_factor.shape[1] - 3 * SHORT
            return jnp.concatenate(pieces + [jnp.zeros((rest, array.shape[1]), array.dtype)], axis=0)

        run(starts(dev_t), short_factor, starts(taper_state))

    @pl.when(jnp.logical_not(few))
    def _():
        run(dev_t, factor, taper_state[...])


def kernel(
    sizes,
    x_hbm,
    col_ref,
    row_ref,
    level_ref,
    field_ref,
    batch_ref,
    value_ref,
    error_ref,
    reach_hbm,
    state,
    dev_t,
    factor,
    taper_state,
    short_factor,
    most,
    x_in,
    near,
    meta,
    taper_obs,
    picked,
    parts,
    drawn,
    places,
    values,
    reach_ref,
    reach_sem,
    place_sem,
    load_sem,
    meta_send,
    meta_recv,
    rs_send,
    rs_recv,
    ag_send,
    ag_recv,
    halo_send,
    halo_recv,
    piece_send,
    piece_recv,
):
    tiles, blocks, fields, members, cols, rows, obs, wide = sizes
    near_obs = dev_t.shape[0]
    cells = cols * rows
    share = members // blocks
    tile = lax.axis_index("tile")
    level = lax.axis_index("blk")
    has_left, has_right = tile > 0, tile < tiles - 1

    barrier = pltpu.get_barrier_semaphore()
    for step in (4, 3, 5, 2, 6, 1, 7):
        pl.semaphore_signal(
            barrier, inc=1, device_id={"blk": lax.rem(level + step, blocks)}, device_id_type=MESH
        )

    @pl.when(has_left)
    def _():
        pl.semaphore_signal(barrier, inc=1, device_id={"tile": tile - 1}, device_id_type=MESH)

    @pl.when(has_right)
    def _():
        pl.semaphore_signal(barrier, inc=1, device_id={"tile": tile + 1}, device_id_type=MESH)

    brought = [
        pltpu.make_async_copy(ref, places.at[i], place_sem.at[i])
        for i, ref in enumerate((col_ref, row_ref, level_ref, field_ref, batch_ref))
    ] + [
        pltpu.make_async_copy(ref, values.at[i], place_sem.at[5 + i])
        for i, ref in enumerate((value_ref, error_ref))
    ]
    reach_copy = pltpu.make_async_copy(reach_hbm, reach_ref, reach_sem)
    reach_copy.start()
    for copy in brought:
        copy.start()
    loads = [
        pltpu.make_async_copy(
            x_hbm.at[pl.ds(f * members * cols, members * cols)],
            x_in.at[pl.ds(f * members * cols, members * cols)],
            load_sem.at[f],
        )
        for f in range(fields)
    ]
    for copy in loads:
        copy.start()

    @pl.when(jnp.logical_not(has_left))
    def _():
        near[:, 0] = jnp.zeros((NBATCH, members, wide), F32)
        meta[0] = jnp.zeros((8, wide), F32)

    @pl.when(jnp.logical_not(has_right))
    def _():
        near[:, 2] = jnp.zeros((NBATCH, members, wide), F32)
        meta[2] = jnp.zeros((8, wide), F32)

    drawn[...] = jnp.zeros_like(drawn)
    for copy in brought:
        copy.wait()
    for i in range(5):
        drawn[i : i + 1, :obs] = (places[i] + (1 if i == 4 else 0)).astype(F32)
    for i in range(2):
        drawn[5 + i : 6 + i, :obs] = values[i]
    unsorted = drawn[...]
    key = sort_key(unsorted[4:5], 1)
    turned = jnp.transpose(jnp.concatenate([unsorted, jnp.zeros((LANES - 8, wide), F32)], axis=0))
    key_column = sort_key(turned[:, 4:5], 0)
    rank = jnp.sum(jnp.where(key < key_column, 1.0, 0.0), axis=1, keepdims=True)
    moved = jnp.where(rank == lax.broadcasted_iota(jnp.int32, (wide, wide), 1).astype(F32), 1.0, 0.0)
    high = unsorted.astype(BF16).astype(F32)
    middle = (unsorted - high).astype(BF16).astype(F32)
    low = unsorted - high - middle
    terms = jnp.concatenate([high, middle, low, jnp.zeros_like(low)], axis=0).astype(BF16)
    terms = dot(terms, moved.astype(BF16))
    meta[1] = terms[:8] + terms[8:16] + terms[16:24]

    def strips(array, send, recv):
        right = pltpu.make_async_remote_copy(
            src_ref=array.at[1],
            dst_ref=array.at[0],
            send_sem=send.at[0],
            recv_sem=recv.at[0],
            device_id={"tile": jnp.minimum(tile + 1, tiles - 1)},
            device_id_type=MESH,
        )
        left = pltpu.make_async_remote_copy(
            src_ref=array.at[1],
            dst_ref=array.at[2],
            send_sem=send.at[1],
            recv_sem=recv.at[1],
            device_id={"tile": jnp.maximum(tile - 1, 0)},
            device_id_type=MESH,
        )
        return right, left

    def strips_start(array, send, recv):
        right, left = strips(array, send, recv)
        pl.when(has_right)(right.start)
        pl.when(has_left)(left.start)

    def strips_arrive(array, send, recv):
        right, left = strips(array, send, recv)
        pl.when(has_left)(right.wait_recv)
        pl.when(has_right)(left.wait_recv)

    def strips_sent(array, send, recv):
        right, left = strips(array, send, recv)
        pl.when(has_right)(right.wait_send)
        pl.when(has_left)(left.wait_send)

    own_col, own_row, own_level, own_field = (meta[1, i : i + 1, :] for i in range(4))
    here = (own_level == level.astype(F32)) & (meta[1, 4:5, :] > 0)
    place = jnp.where(here, (own_col - (tile * cols).astype(F32)) * rows + own_row, -1.0)
    cell_at = lax.broadcasted_iota(jnp.int32, (cells, wide), 0).astype(F32)
    chosen = jnp.where(cell_at == place, 1.0, 0.0).astype(BF16)

    def slab(ref, f):
        return jnp.concatenate(
            [ref[pl.ds(f * members * cols + c, members, stride=cols), :] for c in range(cols)], axis=1
        )

    total = jnp.zeros((3 * members, wide), F32)
    for group in [list(range(fields))]:
        terms = []
        for f in group:
            loads[f].wait()
            x = slab(x_in, f)
            high = x.astype(BF16)
            terms += [high, *split(x - high.astype(F32))]
        found = dot(jnp.concatenate(terms, axis=0), chosen)
        for i, f in enumerate(group):
            part = found[i * 3 * members : (i + 1) * 3 * members]
            total = jnp.where(own_field == float(f), part, total)
    picked[...] = total[:members] + total[members : 2 * members] + total[2 * members :]

    def scatter(step):
        peer = lax.rem(level + step, blocks)
        return pltpu.make_async_remote_copy(
            src_ref=picked.at[pl.ds(pl.multiple_of(peer * share, share), share)],
            dst_ref=parts.at[step],
            send_sem=rs_send.at[step],
            recv_sem=rs_recv.at[step],
            device_id={"blk": peer},
            device_id_type=MESH,
        )

    mine = pl.ds(pl.multiple_of(level * share, share), share)

    def gather(step):
        peer = lax.rem(level + step, blocks)
        return pltpu.make_async_remote_copy(
            src_ref=near.at[0, 1, mine],
            dst_ref=near.at[0, 1, mine],
            send_sem=ag_send.at[step],
            recv_sem=ag_recv.at[step],
            device_id={"blk": peer},
            device_id_type=MESH,
        )

    def gather_arrive(step):
        source = lax.rem(level + blocks - step, blocks)
        at = pl.ds(pl.multiple_of(source * share, share), share)
        pltpu.make_async_remote_copy(
            src_ref=near.at[0, 1, at],
            dst_ref=near.at[0, 1, at],
            send_sem=ag_send.at[step],
            recv_sem=ag_recv.at[step],
            device_id={"blk": source},
            device_id_type=MESH,
        ).wait_recv()

    pl.semaphore_wait(
        barrier, (blocks - 1) + has_left.astype(jnp.int32) + has_right.astype(jnp.int32)
    )
    for step in (4, 3, 5, 2, 6, 1, 7):
        scatter(step).start()
    strips_start(meta, meta_send, meta_recv)

    strips_arrive(meta, meta_send, meta_recv)
    reach_copy.wait()
    reach_here = reach_ref[level].astype(F32) + 1.0
    taper_state[3 * obs :] = jnp.zeros((near_obs - 3 * obs, cells), F32)
    taper_obs[3 * obs :] = jnp.zeros((near_obs - 3 * obs, wide), F32)
    dev_t[3 * obs :] = jnp.zeros((near_obs - 3 * obs, wide), BF16)
    lane_row = lax.broadcasted_iota(jnp.int32, (obs, rows), 1).astype(F32)
    columns = []
    for s in range(3):
        turned = jnp.transpose(
            jnp.concatenate([meta[s], jnp.zeros((LANES - 8, wide), F32)], axis=0)
        )
        columns.append([turned[:obs, i : i + 1] for i in range(3)])
    for s in range(3):
        col, row, lev = columns[s]
        vertical = jnp.maximum(0.0, 1.0 - jnp.abs(level.astype(F32) - lev) / reach_here)
        gap = lane_row - row
        gap = gap * gap
        for c in range(cols):
            across = col - (tile * cols + c).astype(F32)
            close = jnp.maximum(1.0 - (across * across + gap) * (1.0 / (cols * cols)), 0.0)
            taper_state[s * obs : (s + 1) * obs, c * rows : (c + 1) * rows] = close * close * vertical

    for step in range(1, blocks):
        scatter(step).wait_recv()
    summed = picked[mine, :]
    for step in range(1, blocks):
        summed = summed + parts[step]
    near[0, 1, mine, :] = summed
    for step in (4, 3, 5, 2, 6, 1, 7):
        gather(step).start()

    def pieces(source):
        at = pl.ds(pl.multiple_of(source * share, share), share)
        right = pltpu.make_async_remote_copy(
            src_ref=near.at[0, 1, at],
            dst_ref=near.at[0, 0, at],
            send_sem=piece_send.at[0, source],
            recv_sem=piece_recv.at[0, source],
            device_id={"tile": jnp.minimum(tile + 1, tiles - 1)},
            device_id_type=MESH,
        )
        left = pltpu.make_async_remote_copy(
            src_ref=near.at[0, 1, at],
            dst_ref=near.at[0, 2, at],
            send_sem=piece_send.at[1, source],
            recv_sem=piece_recv.at[1, source],
            device_id={"tile": jnp.maximum(tile - 1, 0)},
            device_id_type=MESH,
        )
        return right, left

    def piece_start(source):
        right, left = pieces(source)
        pl.when(has_right)(right.start)
        pl.when(has_left)(left.start)

    piece_start(level)

    reach_own = jnp.zeros((1, wide), F32)
    for k in range(blocks):
        reach_own = jnp.where(own_level == float(k), reach_ref[k].astype(F32), reach_own)
    reach_own = 1.0 / (reach_own + 1.0)
    for s in range(3):
        col, row, lev = columns[s]
        across = col - own_col
        gap = row - own_row
        close = jnp.maximum(1.0 - (across * across + gap * gap) * (1.0 / (cols * cols)), 0.0)
        vertical = jnp.maximum(0.0, 1.0 - jnp.abs(own_level - lev) * reach_own)
        taper_obs[s * obs : (s + 1) * obs] = close * close * vertical

    for step in (1, 7, 2, 6, 3, 5, 4):
        gather_arrive(step)
        piece_start(lax.rem(level + blocks - step, blocks))

    first_half = lax.broadcasted_iota(jnp.int32, (wide, LANES), 1) < members

    def statistics(turn):
        pulls = []
        for s in range(3):
            prior = near[turn, s]
            average = jnp.sum(prior, axis=0, keepdims=True) * (1.0 / members)
            deviation = prior - average
            flag = meta[s, 4:5, :]
            error = jnp.where(flag > 0, meta[s, 6:7, :], 1.0)
            spread = jnp.sum(deviation * deviation, axis=0, keepdims=True) * (1.0 / (members - 1)) + error
            shrink = 1.0 / (1.0 + jnp.sqrt(error / spread))
            innovation = meta[s, 5:6, :] - average
            coefficient = jnp.where(flag == jnp.asarray(turn + 1, F32), 1.0 / (spread * (members - 1)), 0.0)
            weighted = deviation * coefficient
            turned = jnp.transpose(jnp.concatenate([weighted, weighted], axis=0))
            high = turned.astype(BF16).astype(F32)
            both = jnp.where(first_half, high, turned - high).astype(BF16)[:obs]
            dev_t[s * obs : (s + 1) * obs] = jnp.concatenate([both, both], axis=1)
            pulls.append((innovation - shrink * deviation)[:, :obs])
        factor[...] = side_by_side(pulls, near_obs)
        return pulls

    for f in range(fields):
        state[f] = slab(x_in, f)
    for source in range(blocks):
        right, left = pieces(source)
        pl.when(has_left)(right.wait_recv)
        pl.when(has_right)(left.wait_recv)

    def batch(turn, carry):
        statistics(turn)
        near[turn + 1, 1] = update(near[turn, 1], dev_t, factor, taper_obs[...])
        strips_start(near.at[turn + 1], halo_send.at[turn + 1], halo_recv.at[turn + 1])
        for group in groups(fields):
            xs = [state[f] for f in group]
            for f, x in zip(group, update_fields(xs, dev_t, factor, taper_state[...])):
                state[f] = x
        strips_arrive(near.at[turn + 1], halo_send.at[turn + 1], halo_recv.at[turn + 1])
        return carry

    lax.fori_loop(0, NBATCH - 1, batch, 0)
    pulls = statistics(NBATCH - 1)
    short_factor[...] = side_by_side([pull[:, :SHORT] for pull in pulls], wide)
    counts = [
        jnp.sum(jnp.where(meta[s, 4:5, :] == float(NBATCH), 1.0, 0.0), axis=1, keepdims=True)
        for s in range(3)
    ]
    most[...] = jnp.broadcast_to(functools.reduce(jnp.maximum, counts), (8, LANES))

    strips_sent(meta, meta_send, meta_recv)
    for step in range(1, blocks):
        scatter(step).wait_send()
        gather(step).wait_send()
    for source in range(blocks):
        right, left = pieces(source)
        pl.when(has_right)(right.wait_send)
        pl.when(has_left)(left.wait_send)
    for turn in range(1, NBATCH):
        strips_sent(near.at[turn], halo_send.at[turn], halo_recv.at[turn])


def shards(
    tiles, blocks, ensemble, obs_col, obs_row, obs_level, obs_field, obs_batch, obs_value, obs_error, band_reach
):
    levels, fields, members, cols, rows = ensemble.shape
    obs = obs_col.shape[0]
    wide = 256
    cells = cols * rows
    sizes = (tiles, blocks, fields, members, cols, rows, obs, wide)
    any_space = pl.BlockSpec(memory_space=pltpu.HBM)
    vmem = pl.BlockSpec(memory_space=pltpu.VMEM)
    in_hbm = functools.partial(pltpu.with_memory_space_constraint, memory_space=pltpu.HBM)
    flat = fields * members * cols
    near_obs = -(-3 * obs // 32) * 32
    made = pl.pallas_call(
        functools.partial(kernel, sizes),
        out_shape=(
            jax.ShapeDtypeStruct((fields, members, cells), F32),
            jax.ShapeDtypeStruct((near_obs, wide), BF16),
            jax.ShapeDtypeStruct((2 * members, near_obs), BF16),
            jax.ShapeDtypeStruct((near_obs, cells), F32),
            jax.ShapeDtypeStruct((2 * members, wide), BF16),
            jax.ShapeDtypeStruct((8, LANES), F32),
        ),
        in_specs=[any_space] * 9,
        out_specs=[vmem] * 6,
        scratch_shapes=[
            pltpu.VMEM((flat, rows), F32),
            pltpu.VMEM((NBATCH, 3, members, wide), F32),
            pltpu.VMEM((3, 8, wide), F32),
            pltpu.VMEM((near_obs, wide), F32),
            pltpu.VMEM((members, wide), F32),
            pltpu.VMEM((blocks, members // blocks, wide), F32),
            pltpu.VMEM((8, wide), F32),
            pltpu.VMEM((5, 1, obs), jnp.int32),
            pltpu.VMEM((2, 1, obs), F32),
            pltpu.SMEM((blocks,), jnp.int32),
            pltpu.SemaphoreType.DMA,
            pltpu.SemaphoreType.DMA((7,)),
            pltpu.SemaphoreType.DMA((fields,)),
            pltpu.SemaphoreType.DMA((2,)),
            pltpu.SemaphoreType.DMA((2,)),
            pltpu.SemaphoreType.DMA((blocks,)),
            pltpu.SemaphoreType.DMA((blocks,)),
            pltpu.SemaphoreType.DMA((blocks,)),
            pltpu.SemaphoreType.DMA((blocks,)),
            pltpu.SemaphoreType.DMA((NBATCH, 2)),
            pltpu.SemaphoreType.DMA((NBATCH, 2)),
            pltpu.SemaphoreType.DMA((2, blocks)),
            pltpu.SemaphoreType.DMA((2, blocks)),
        ],
        compiler_params=pltpu.CompilerParams(
            collective_id=0, has_side_effects=True, vmem_limit_bytes=VMEM_LIMIT * 2**20
        ),
    )(
        in_hbm(ensemble.reshape(flat, rows)),
        *(
            in_hbm(v.reshape(1, obs))
            for v in (obs_col, obs_row, obs_level, obs_field, obs_batch, obs_value, obs_error)
        ),
        in_hbm(band_reach),
    )
    out = pl.pallas_call(
        functools.partial(finish, (fields, members, cols, rows, obs)),
        out_shape=jax.ShapeDtypeStruct((flat, rows), F32),
        in_specs=[vmem] * 6,
        out_specs=any_space,
        scratch_shapes=[pltpu.VMEM((flat, rows), F32), pltpu.SemaphoreType.DMA((fields,))],
        compiler_params=pltpu.CompilerParams(vmem_limit_bytes=VMEM_LIMIT * 2**20),
    )(*made)
    return out.reshape(levels, fields, members, cols, rows)


def solution(mesh):
    return jax.shard_map(
        functools.partial(shards, mesh.shape["tile"], mesh.shape["blk"]),
        mesh=mesh,
        in_specs=(
            P("blk", None, None, "tile", None),
            P("tile"),
            P("tile"),
            P("tile"),
            P("tile"),
            P("tile"),
            P("tile"),
            P("tile"),
            P(),
        ),
        out_specs=P("blk", None, None, "tile", None),
        check_vma=False,
    )
```

```python
import functools

import jax
import jax.numpy as jnp
from jax import lax
from jax.experimental import pallas as pl
from jax.experimental.pallas import tpu as pltpu
from jax.sharding import PartitionSpec as P

MESH = pl.DeviceIdType.MESH
NBATCH = 4
F32 = jnp.float32
BF16 = jnp.bfloat16
LANES = 128
VMEM_LIMIT = 24
SHORT = 80


def split(x):
    high = x.astype(BF16)
    low = (x - high.astype(F32)).astype(BF16)
    return high, low


def sort_key(flag, axis):
    turn = jnp.where(flag > 0, NBATCH - flag, float(NBATCH))
    at = lax.broadcasted_iota(jnp.int32, flag.shape, axis).astype(F32)
    return turn * float(flag.shape[axis]) + at


def dot(a, b):
    return jnp.dot(a, b, preferred_element_type=F32)


def side_by_side(pulls, width):
    have = sum(pull.shape[1] for pull in pulls)
    pulls = pulls + [jnp.zeros((pulls[0].shape[0], width - have), F32)]
    high, low = split(jnp.concatenate(pulls, axis=1))
    return jnp.concatenate([high, low], axis=0)


def update(x, dev_t, factor, taper):
    members = x.shape[0]
    high, low = split(x)
    stacked = jnp.concatenate([high, high, low, low], axis=0)
    gain_high, gain_low = split(dot(dev_t[...], stacked) * taper)
    both = dot(factor[...], gain_high)
    return x + (both[:members] + both[members:] + dot(factor[:members], gain_low))


def groups(fields):
    return [list(range(f, min(f + 2, fields))) for f in range(0, fields, 2)]


def finish(sizes, state, dev_t, factor, taper_state, short_factor, most, out_hbm, out, out_sem):
    fields, members, cols, rows, obs = sizes
    flat = members * cols

    def run(dev, pull, taper):
        taper = jnp.concatenate(
            [taper[:, c * rows : (c + 1) * rows] for c in range(cols) for f in range(fields)], axis=1
        )
        x = update(state[...], dev, pull, taper)
        copies = []
        for f in range(fields):
            for c in range(cols):
                at = (c * fields + f) * rows
                out[pl.ds(f * flat + c, members, stride=cols), :] = x[:, at : at + rows]
            part = pl.ds(f * flat, flat)
            copies.append(pltpu.make_async_copy(out.at[part], out_hbm.at[part], out_sem.at[f]))
            copies[-1].start()
        for copy in copies:
            copy.wait()

    few = jnp.max(most[...]) <= float(SHORT)

    @pl.when(few)
    def _():
        def starts(array):
            pieces = [array[s * obs : s * obs + SHORT] for s in range(3)]
            rest = short_factor.shape[1] - 3 * SHORT
            return jnp.concatenate(pieces + [jnp.zeros((rest, array.shape[1]), array.dtype)], axis=0)

        run(starts(dev_t), short_factor, starts(taper_state))

    @pl.when(jnp.logical_not(few))
    def _():
        run(dev_t, factor, taper_state[...])


def kernel(
    sizes,
    x_hbm,
    col_ref,
    row_ref,
    level_ref,
    field_ref,
    batch_ref,
    value_ref,
    error_ref,
    reach_hbm,
    state,
    dev_t,
    factor,
    taper_state,
    short_factor,
    most,
    x_in,
    near,
    meta,
    taper_obs,
    picked,
    parts,
    right_factor,
    drawn,
    places,
    values,
    reach_ref,
    reach_sem,
    place_sem,
    load_sem,
    meta_send,
    meta_recv,
    rs_send,
    rs_recv,
    ag_send,
    ag_recv,
    halo_send,
    halo_recv,
    piece_send,
    piece_recv,
):
    tiles, blocks, fields, members, cols, rows, obs, wide = sizes
    near_obs = dev_t.shape[0]
    cells = cols * rows

    def block(s):
        return slice(s * obs, (s + 1) * obs)

    share = members // blocks
    tile = lax.axis_index("tile")
    level = lax.axis_index("blk")
    has_left, has_right = tile > 0, tile < tiles - 1

    barrier = pltpu.get_barrier_semaphore()
    for step in (4, 3, 5, 2, 6, 1, 7):
        pl.semaphore_signal(
            barrier, inc=1, device_id={"blk": lax.rem(level + step, blocks)}, device_id_type=MESH
        )

    @pl.when(has_left)
    def _():
        pl.semaphore_signal(barrier, inc=1, device_id={"tile": tile - 1}, device_id_type=MESH)

    @pl.when(has_right)
    def _():
        pl.semaphore_signal(barrier, inc=1, device_id={"tile": tile + 1}, device_id_type=MESH)

    brought = [
        pltpu.make_async_copy(ref, places.at[i], place_sem.at[i])
        for i, ref in enumerate((col_ref, row_ref, level_ref, field_ref, batch_ref))
    ] + [
        pltpu.make_async_copy(ref, values.at[i], place_sem.at[5 + i])
        for i, ref in enumerate((value_ref, error_ref))
    ]
    reach_copy = pltpu.make_async_copy(reach_hbm, reach_ref, reach_sem)
    reach_copy.start()
    for copy in brought:
        copy.start()
    loads = [
        pltpu.make_async_copy(
            x_hbm.at[pl.ds(f * members * cols, members * cols)],
            x_in.at[pl.ds(f * members * cols, members * cols)],
            load_sem.at[f],
        )
        for f in range(fields)
    ]
    for copy in loads:
        copy.start()

    @pl.when(jnp.logical_not(has_left))
    def _():
        near[:, 0] = jnp.zeros((NBATCH, members, wide), F32)
        meta[0] = jnp.zeros((8, wide), F32)

    @pl.when(jnp.logical_not(has_right))
    def _():
        near[:, 2] = jnp.zeros((NBATCH, members, wide), F32)
        meta[2] = jnp.zeros((8, wide), F32)

    drawn[...] = jnp.zeros_like(drawn)
    for copy in brought:
        copy.wait()
    for i in range(5):
        drawn[i : i + 1, :obs] = (places[i] + (1 if i == 4 else 0)).astype(F32)
    for i in range(2):
        drawn[5 + i : 6 + i, :obs] = values[i]
    unsorted = drawn[...]
    key = sort_key(unsorted[4:5], 1)
    turned = jnp.transpose(jnp.concatenate([unsorted, jnp.zeros((LANES - 8, wide), F32)], axis=0))
    key_column = sort_key(turned[:, 4:5], 0)
    rank = jnp.sum(jnp.where(key < key_column, 1.0, 0.0), axis=1, keepdims=True)
    moved = jnp.where(rank == lax.broadcasted_iota(jnp.int32, (wide, wide), 1).astype(F32), 1.0, 0.0)
    high = unsorted.astype(BF16).astype(F32)
    middle = (unsorted - high).astype(BF16).astype(F32)
    low = unsorted - high - middle
    terms = jnp.concatenate([high, middle, low, jnp.zeros_like(low)], axis=0).astype(BF16)
    terms = dot(terms, moved.astype(BF16))
    meta[1] = terms[:8] + terms[8:16] + terms[16:24]

    def strips(array, send, recv):
        right = pltpu.make_async_remote_copy(
            src_ref=array.at[1],
            dst_ref=array.at[0],
            send_sem=send.at[0],
            recv_sem=recv.at[0],
            device_id={"tile": jnp.minimum(tile + 1, tiles - 1)},
            device_id_type=MESH,
        )
        left = pltpu.make_async_remote_copy(
            src_ref=array.at[1],
            dst_ref=array.at[2],
            send_sem=send.at[1],
            recv_sem=recv.at[1],
            device_id={"tile": jnp.maximum(tile - 1, 0)},
            device_id_type=MESH,
        )
        return right, left

    def strips_start(array, send, recv):
        right, left = strips(array, send, recv)
        pl.when(has_right)(right.start)
        pl.when(has_left)(left.start)

    def strips_arrive(array, send, recv):
        right, left = strips(array, send, recv)
        pl.when(has_left)(right.wait_recv)
        pl.when(has_right)(left.wait_recv)

    def strips_sent(array, send, recv):
        right, left = strips(array, send, recv)
        pl.when(has_right)(right.wait_send)
        pl.when(has_left)(left.wait_send)

    own_col, own_row, own_level, own_field = (meta[1, i : i + 1, :] for i in range(4))
    here = (own_level == level.astype(F32)) & (meta[1, 4:5, :] > 0)
    place = jnp.where(here, (own_col - (tile * cols).astype(F32)) * rows + own_row, -1.0)
    cell_at = lax.broadcasted_iota(jnp.int32, (cells, wide), 0).astype(F32)
    chosen = jnp.where(cell_at == place, 1.0, 0.0).astype(BF16)

    def slab(ref, f):
        return jnp.concatenate(
            [ref[pl.ds(f * members * cols + c, members, stride=cols), :] for c in range(cols)], axis=1
        )

    total = jnp.zeros((3 * members, wide), F32)
    for group in [list(range(fields))]:
        terms = []
        for f in group:
            loads[f].wait()
            x = slab(x_in, f)
            high = x.astype(BF16)
            terms += [high, *split(x - high.astype(F32))]
        found = dot(jnp.concatenate(terms, axis=0), chosen)
        for i, f in enumerate(group):
            part = found[i * 3 * members : (i + 1) * 3 * members]
            total = jnp.where(own_field == float(f), part, total)
    picked[...] = total[:members] + total[members : 2 * members] + total[2 * members :]

    def scatter(step):
        peer = lax.rem(level + step, blocks)
        return pltpu.make_async_remote_copy(
            src_ref=picked.at[pl.ds(pl.multiple_of(peer * share, share), share)],
            dst_ref=parts.at[step],
            send_sem=rs_send.at[step],
            recv_sem=rs_recv.at[step],
            device_id={"blk": peer},
            device_id_type=MESH,
        )

    mine = pl.ds(pl.multiple_of(level * share, share), share)

    def gather(step):
        peer = lax.rem(level + step, blocks)
        return pltpu.make_async_remote_copy(
            src_ref=near.at[0, 1, mine],
            dst_ref=near.at[0, 1, mine],
            send_sem=ag_send.at[step],
            recv_sem=ag_recv.at[step],
            device_id={"blk": peer},
            device_id_type=MESH,
        )

    def gather_arrive(step):
        source = lax.rem(level + blocks - step, blocks)
        at = pl.ds(pl.multiple_of(source * share, share), share)
        pltpu.make_async_remote_copy(
            src_ref=near.at[0, 1, at],
            dst_ref=near.at[0, 1, at],
            send_sem=ag_send.at[step],
            recv_sem=ag_recv.at[step],
            device_id={"blk": source},
            device_id_type=MESH,
        ).wait_recv()

    pl.semaphore_wait(
        barrier, (blocks - 1) + has_left.astype(jnp.int32) + has_right.astype(jnp.int32)
    )
    for step in (4, 3, 5, 2, 6, 1, 7):
        scatter(step).start()
    strips_start(meta, meta_send, meta_recv)

    strips_arrive(meta, meta_send, meta_recv)
    reach_copy.wait()
    reach_here = reach_ref[level].astype(F32) + 1.0
    taper_state[3 * obs :] = jnp.zeros((near_obs - 3 * obs, cells), F32)
    taper_obs[3 * obs :] = jnp.zeros((near_obs - 3 * obs, wide), F32)
    dev_t[3 * obs :] = jnp.zeros((near_obs - 3 * obs, wide), BF16)
    lane_row = lax.broadcasted_iota(jnp.int32, (obs, rows), 1).astype(F32)
    columns = []
    for s in range(3):
        turned = jnp.transpose(
            jnp.concatenate([meta[s], jnp.zeros((LANES - 8, wide), F32)], axis=0)
        )
        columns.append([turned[:obs, i : i + 1] for i in range(3)])
    for s in range(3):
        col, row, lev = columns[s]
        vertical = jnp.maximum(0.0, 1.0 - jnp.abs(level.astype(F32) - lev) / reach_here)
        gap = lane_row - row
        gap = gap * gap
        for c in range(cols):
            across = col - (tile * cols + c).astype(F32)
            close = jnp.maximum(1.0 - (across * across + gap) * (1.0 / (cols * cols)), 0.0)
            taper_state[block(s), c * rows : (c + 1) * rows] = close * close * vertical

    for step in range(1, blocks):
        scatter(step).wait_recv()
    summed = picked[mine, :]
    for step in range(1, blocks):
        summed = summed + parts[step]
    near[0, 1, mine, :] = summed
    for step in (4, 3, 5, 2, 6, 1, 7):
        gather(step).start()

    def pieces(source):
        at = pl.ds(pl.multiple_of(source * share, share), share)
        right = pltpu.make_async_remote_copy(
            src_ref=near.at[0, 1, at],
            dst_ref=near.at[0, 0, at],
            send_sem=piece_send.at[0, source],
            recv_sem=piece_recv.at[0, source],
            device_id={"tile": jnp.minimum(tile + 1, tiles - 1)},
            device_id_type=MESH,
        )
        left = pltpu.make_async_remote_copy(
            src_ref=near.at[0, 1, at],
            dst_ref=near.at[0, 2, at],
            send_sem=piece_send.at[1, source],
            recv_sem=piece_recv.at[1, source],
            device_id={"tile": jnp.maximum(tile - 1, 0)},
            device_id_type=MESH,
        )
        return right, left

    def piece_start(source):
        right, left = pieces(source)
        pl.when(has_right)(right.start)
        pl.when(has_left)(left.start)

    piece_start(level)

    reach_own = jnp.zeros((1, wide), F32)
    for k in range(blocks):
        reach_own = jnp.where(own_level == float(k), reach_ref[k].astype(F32), reach_own)
    reach_own = 1.0 / (reach_own + 1.0)
    for s in range(3):
        col, row, lev = columns[s]
        across = col - own_col
        gap = row - own_row
        close = jnp.maximum(1.0 - (across * across + gap * gap) * (1.0 / (cols * cols)), 0.0)
        vertical = jnp.maximum(0.0, 1.0 - jnp.abs(own_level - lev) * reach_own)
        taper_obs[block(s)] = close * close * vertical

    for step in (1, 7, 2, 6, 3, 5, 4):
        gather_arrive(step)
        piece_start(lax.rem(level + blocks - step, blocks))

    first_half = lax.broadcasted_iota(jnp.int32, (wide, LANES), 1) < members

    def statistics(turn, s):
        prior = near[turn, s]
        average = jnp.sum(prior, axis=0, keepdims=True) * (1.0 / members)
        deviation = prior - average
        flag = meta[s, 4:5, :]
        error = jnp.where(flag > 0, meta[s, 6:7, :], 1.0)
        spread = jnp.sum(deviation * deviation, axis=0, keepdims=True) * (1.0 / (members - 1)) + error
        shrink = 1.0 / (1.0 + jnp.sqrt(error / spread))
        innovation = meta[s, 5:6, :] - average
        coefficient = jnp.where(flag == jnp.asarray(turn + 1, F32), 1.0 / (spread * (members - 1)), 0.0)
        weighted = deviation * coefficient
        turned = jnp.transpose(jnp.concatenate([weighted, weighted], axis=0))
        high = turned.astype(BF16).astype(F32)
        both = jnp.where(first_half, high, turned - high).astype(BF16)[:obs]
        dev_t[block(s)] = jnp.concatenate([both, both], axis=1)
        return innovation - shrink * deviation

    for c in range(cols):
        for f in range(fields):
            state[:, (c * fields + f) * rows : (c * fields + f + 1) * rows] = x_in[
                pl.ds(f * members * cols + c, members, stride=cols), :
            ]
    for source in range(blocks):
        right, left = pieces(source)
        pl.when(has_left)(right.wait_recv)
        pl.when(has_right)(left.wait_recv)

    def batch(turn, carry):
        pulls = [statistics(turn, s)[:, :obs] for s in range(3)]
        factor[...] = side_by_side(pulls, near_obs)
        near[turn + 1, 1] = update(near[turn, 1], dev_t, factor, taper_obs[...])
        strips_start(near.at[turn + 1], halo_send.at[turn + 1], halo_recv.at[turn + 1])
        right_factor[...] = side_by_side(pulls[1:], near_obs - obs)
        for first, last, begin, end, pull in (
            (0, 1, 0, 2 * obs, factor[:, : 2 * obs]),
            (1, cols - 1, 0, near_obs, factor),
            (cols - 1, cols, obs, near_obs, right_factor),
        ):
            at = slice(first * fields * rows, last * fields * rows)
            taper = jnp.concatenate(
                [
                    taper_state[begin:end, c * rows : (c + 1) * rows]
                    for c in range(first, last)
                    for f in range(fields)
                ],
                axis=1,
            )
            state[:, at] = update(state[:, at], dev_t[begin:end], pull, taper)
        strips_arrive(near.at[turn + 1], halo_send.at[turn + 1], halo_recv.at[turn + 1])
        return carry

    lax.fori_loop(0, NBATCH - 1, batch, 0)
    pulls = [statistics(NBATCH - 1, s)[:, :obs] for s in range(3)]
    factor[...] = side_by_side(pulls, near_obs)
    short_factor[...] = side_by_side([pull[:, :SHORT] for pull in pulls], wide)
    counts = [
        jnp.sum(jnp.where(meta[s, 4:5, :] == float(NBATCH), 1.0, 0.0), axis=1, keepdims=True)
        for s in range(3)
    ]
    most[...] = jnp.broadcast_to(functools.reduce(jnp.maximum, counts), (8, LANES))

    strips_sent(meta, meta_send, meta_recv)
    for step in range(1, blocks):
        scatter(step).wait_send()
        gather(step).wait_send()
    for source in range(blocks):
        right, left = pieces(source)
        pl.when(has_right)(right.wait_send)
        pl.when(has_left)(left.wait_send)
    for turn in range(1, NBATCH):
        strips_sent(near.at[turn], halo_send.at[turn], halo_recv.at[turn])


def shards(
    tiles, blocks, ensemble, obs_col, obs_row, obs_level, obs_field, obs_batch, obs_value, obs_error, band_reach
):
    levels, fields, members, cols, rows = ensemble.shape
    obs = obs_col.shape[0]
    wide = 256
    cells = cols * rows
    sizes = (tiles, blocks, fields, members, cols, rows, obs, wide)
    any_space = pl.BlockSpec(memory_space=pltpu.HBM)
    vmem = pl.BlockSpec(memory_space=pltpu.VMEM)
    in_hbm = functools.partial(pltpu.with_memory_space_constraint, memory_space=pltpu.HBM)
    flat = fields * members * cols
    near_obs = -(-3 * obs // 32) * 32
    made = pl.pallas_call(
        functools.partial(kernel, sizes),
        out_shape=(
            jax.ShapeDtypeStruct((members, fields * cells), F32),
            jax.ShapeDtypeStruct((near_obs, wide), BF16),
            jax.ShapeDtypeStruct((2 * members, near_obs), BF16),
            jax.ShapeDtypeStruct((near_obs, cells), F32),
            jax.ShapeDtypeStruct((2 * members, wide), BF16),
            jax.ShapeDtypeStruct((8, LANES), F32),
        ),
        in_specs=[any_space] * 9,
        out_specs=[vmem] * 6,
        scratch_shapes=[
            pltpu.VMEM((flat, rows), F32),
            pltpu.VMEM((NBATCH, 3, members, wide), F32),
            pltpu.VMEM((3, 8, wide), F32),
            pltpu.VMEM((near_obs, wide), F32),
            pltpu.VMEM((members, wide), F32),
            pltpu.VMEM((blocks, members // blocks, wide), F32),
            pltpu.VMEM((2 * members, near_obs - obs), BF16),
            pltpu.VMEM((8, wide), F32),
            pltpu.VMEM((5, 1, obs), jnp.int32),
            pltpu.VMEM((2, 1, obs), F32),
            pltpu.SMEM((blocks,), jnp.int32),
            pltpu.SemaphoreType.DMA,
            pltpu.SemaphoreType.DMA((7,)),
            pltpu.SemaphoreType.DMA((fields,)),
            pltpu.SemaphoreType.DMA((2,)),
            pltpu.SemaphoreType.DMA((2,)),
            pltpu.SemaphoreType.DMA((blocks,)),
            pltpu.SemaphoreType.DMA((blocks,)),
            pltpu.SemaphoreType.DMA((blocks,)),
            pltpu.SemaphoreType.DMA((blocks,)),
            pltpu.SemaphoreType.DMA((NBATCH, 2)),
            pltpu.SemaphoreType.DMA((NBATCH, 2)),
            pltpu.SemaphoreType.DMA((2, blocks)),
            pltpu.SemaphoreType.DMA((2, blocks)),
        ],
        compiler_params=pltpu.CompilerParams(
            collective_id=0, has_side_effects=True, vmem_limit_bytes=VMEM_LIMIT * 2**20
        ),
    )(
        in_hbm(ensemble.reshape(flat, rows)),
        *(
            in_hbm(v.reshape(1, obs))
            for v in (obs_col, obs_row, obs_level, obs_field, obs_batch, obs_value, obs_error)
        ),
        in_hbm(band_reach),
    )
    out = pl.pallas_call(
        functools.partial(finish, (fields, members, cols, rows, obs)),
        out_shape=jax.ShapeDtypeStruct((flat, rows), F32),
        in_specs=[vmem] * 6,
        out_specs=any_space,
        scratch_shapes=[pltpu.VMEM((flat, rows), F32), pltpu.SemaphoreType.DMA((fields,))],
        compiler_params=pltpu.CompilerParams(vmem_limit_bytes=VMEM_LIMIT * 2**20),
    )(*made)
    return out.reshape(levels, fields, members, cols, rows)


def solution(mesh):
    return jax.shard_map(
        functools.partial(shards, mesh.shape["tile"], mesh.shape["blk"]),
        mesh=mesh,
        in_specs=(
            P("blk", None, None, "tile", None),
            P("tile"),
            P("tile"),
            P("tile"),
            P("tile"),
            P("tile"),
            P("tile"),
            P("tile"),
            P(),
        ),
        out_specs=P("blk", None, None, "tile", None),
        check_vma=False,
    )
```

```python
import functools

import jax
import jax.numpy as jnp
from jax import lax
from jax.experimental import pallas as pl
from jax.experimental.pallas import tpu as pltpu
from jax.sharding import PartitionSpec as P

MESH = pl.DeviceIdType.MESH
NBATCH = 4
F32 = jnp.float32
BF16 = jnp.bfloat16
LANES = 128
VMEM_LIMIT = 24
SHORT = 80


def split(x):
    high = x.astype(BF16)
    low = (x - high.astype(F32)).astype(BF16)
    return high, low


def sort_key(flag, axis):
    turn = jnp.where(flag > 0, NBATCH - flag, float(NBATCH))
    at = lax.broadcasted_iota(jnp.int32, flag.shape, axis).astype(F32)
    return turn * float(flag.shape[axis]) + at


def dot(a, b):
    return jnp.dot(a, b, preferred_element_type=F32)


def side_by_side(pulls, width):
    have = sum(pull.shape[1] for pull in pulls)
    pulls = pulls + [jnp.zeros((pulls[0].shape[0], width - have), F32)]
    high, low = split(jnp.concatenate(pulls, axis=1))
    return jnp.concatenate([high, low], axis=0)


def update(x, dev_t, factor, taper):
    members = x.shape[0]
    high, low = split(x)
    stacked = jnp.concatenate([high, high, low, low], axis=0)
    gain_high, gain_low = split(dot(dev_t[...], stacked) * taper)
    both = dot(factor[...], gain_high)
    return x + (both[:members] + both[members:] + dot(factor[:members], gain_low))


def groups(fields):
    return [list(range(f, min(f + 2, fields))) for f in range(0, fields, 2)]


def finish(sizes, state, dev_t, factor, taper_state, short_factor, most, out_hbm, out, out_sem):
    fields, members, cols, rows, obs = sizes
    flat = members * cols

    def run(dev, pull, taper):
        taper = jnp.concatenate(
            [taper[:, c * rows : (c + 1) * rows] for c in range(cols) for f in range(fields)], axis=1
        )
        x = update(state[...], dev, pull, taper)
        copies = []
        for f in range(fields):
            for c in range(cols):
                at = (c * fields + f) * rows
                out[pl.ds(f * flat + c, members, stride=cols), :] = x[:, at : at + rows]
            part = pl.ds(f * flat, flat)
            copies.append(pltpu.make_async_copy(out.at[part], out_hbm.at[part], out_sem.at[f]))
            copies[-1].start()
        for copy in copies:
            copy.wait()

    few = jnp.max(most[...]) <= float(SHORT)

    @pl.when(few)
    def _():
        def starts(array):
            pieces = [array[s * obs : s * obs + SHORT] for s in range(3)]
            rest = short_factor.shape[1] - 3 * SHORT
            return jnp.concatenate(pieces + [jnp.zeros((rest, array.shape[1]), array.dtype)], axis=0)

        run(starts(dev_t), short_factor, starts(taper_state))

    @pl.when(jnp.logical_not(few))
    def _():
        run(dev_t, factor, taper_state[...])


def kernel(
    sizes,
    x_hbm,
    col_ref,
    row_ref,
    level_ref,
    field_ref,
    batch_ref,
    value_ref,
    error_ref,
    reach_hbm,
    state,
    dev_t,
    factor,
    taper_state,
    short_factor,
    most,
    x_in,
    near,
    meta,
    taper_obs,
    picked,
    parts,
    right_factor,
    drawn,
    places,
    values,
    reach_ref,
    reach_sem,
    place_sem,
    load_sem,
    meta_send,
    meta_recv,
    rs_send,
    rs_recv,
    ag_send,
    ag_recv,
    halo_send,
    halo_recv,
    piece_send,
    piece_recv,
):
    tiles, blocks, fields, members, cols, rows, obs, wide = sizes
    near_obs = dev_t.shape[0]
    cells = cols * rows

    def block(s):
        return slice(s * obs, (s + 1) * obs)

    share = members // blocks
    tile = lax.axis_index("tile")
    level = lax.axis_index("blk")
    has_left, has_right = tile > 0, tile < tiles - 1

    barrier = pltpu.get_barrier_semaphore()
    for step in (4, 3, 5, 2, 6, 1, 7):
        pl.semaphore_signal(
            barrier, inc=1, device_id={"blk": lax.rem(level + step, blocks)}, device_id_type=MESH
        )

    @pl.when(has_left)
    def _():
        pl.semaphore_signal(barrier, inc=1, device_id={"tile": tile - 1}, device_id_type=MESH)

    @pl.when(has_right)
    def _():
        pl.semaphore_signal(barrier, inc=1, device_id={"tile": tile + 1}, device_id_type=MESH)

    brought = [
        pltpu.make_async_copy(ref, places.at[i], place_sem.at[i])
        for i, ref in enumerate((col_ref, row_ref, level_ref, field_ref, batch_ref))
    ] + [
        pltpu.make_async_copy(ref, values.at[i], place_sem.at[5 + i])
        for i, ref in enumerate((value_ref, error_ref))
    ]
    reach_copy = pltpu.make_async_copy(reach_hbm, reach_ref, reach_sem)
    reach_copy.start()
    for copy in brought:
        copy.start()
    loads = [
        pltpu.make_async_copy(
            x_hbm.at[pl.ds(f * members * cols, members * cols)],
            x_in.at[pl.ds(f * members * cols, members * cols)],
            load_sem.at[f],
        )
        for f in range(fields)
    ]
    for copy in loads:
        copy.start()

    @pl.when(jnp.logical_not(has_left))
    def _():
        near[:, 0] = jnp.zeros((NBATCH, members, wide), F32)
        meta[0] = jnp.zeros((8, wide), F32)

    @pl.when(jnp.logical_not(has_right))
    def _():
        near[:, 2] = jnp.zeros((NBATCH, members, wide), F32)
        meta[2] = jnp.zeros((8, wide), F32)

    drawn[...] = jnp.zeros_like(drawn)
    for copy in brought:
        copy.wait()
    for i in range(5):
        drawn[i : i + 1, :obs] = (places[i] + (1 if i == 4 else 0)).astype(F32)
    for i in range(2):
        drawn[5 + i : 6 + i, :obs] = values[i]
    unsorted = drawn[...]
    key = sort_key(unsorted[4:5], 1)
    turned = jnp.transpose(jnp.concatenate([unsorted, jnp.zeros((LANES - 8, wide), F32)], axis=0))
    key_column = sort_key(turned[:, 4:5], 0)
    rank = jnp.sum(jnp.where(key < key_column, 1.0, 0.0), axis=1, keepdims=True)
    moved = jnp.where(rank == lax.broadcasted_iota(jnp.int32, (wide, wide), 1).astype(F32), 1.0, 0.0)
    high = unsorted.astype(BF16).astype(F32)
    middle = (unsorted - high).astype(BF16).astype(F32)
    low = unsorted - high - middle
    terms = jnp.concatenate([high, middle, low, jnp.zeros_like(low)], axis=0).astype(BF16)
    terms = dot(terms, moved.astype(BF16))
    meta[1] = terms[:8] + terms[8:16] + terms[16:24]

    def strips(array, send, recv):
        right = pltpu.make_async_remote_copy(
            src_ref=array.at[1],
            dst_ref=array.at[0],
            send_sem=send.at[0],
            recv_sem=recv.at[0],
            device_id={"tile": jnp.minimum(tile + 1, tiles - 1)},
            device_id_type=MESH,
        )
        left = pltpu.make_async_remote_copy(
            src_ref=array.at[1],
            dst_ref=array.at[2],
            send_sem=send.at[1],
            recv_sem=recv.at[1],
            device_id={"tile": jnp.maximum(tile - 1, 0)},
            device_id_type=MESH,
        )
        return right, left

    def strips_start(array, send, recv):
        right, left = strips(array, send, recv)
        pl.when(has_right)(right.start)
        pl.when(has_left)(left.start)

    def strips_arrive(array, send, recv):
        right, left = strips(array, send, recv)
        pl.when(has_left)(right.wait_recv)
        pl.when(has_right)(left.wait_recv)

    def strips_sent(array, send, recv):
        right, left = strips(array, send, recv)
        pl.when(has_right)(right.wait_send)
        pl.when(has_left)(left.wait_send)

    own_col, own_row, own_level, own_field = (meta[1, i : i + 1, :] for i in range(4))
    here = (own_level == level.astype(F32)) & (meta[1, 4:5, :] > 0)
    place = jnp.where(here, (own_col - (tile * cols).astype(F32)) * rows + own_row, -1.0)
    cell_at = lax.broadcasted_iota(jnp.int32, (cells, wide), 0).astype(F32)
    chosen = jnp.where(cell_at == place, 1.0, 0.0).astype(BF16)

    def slab(ref, f):
        return jnp.concatenate(
            [ref[pl.ds(f * members * cols + c, members, stride=cols), :] for c in range(cols)], axis=1
        )

    total = jnp.zeros((3 * members, wide), F32)
    for group in [list(range(fields))]:
        terms = []
        for f in group:
            loads[f].wait()
            x = slab(x_in, f)
            high = x.astype(BF16)
            terms += [high, *split(x - high.astype(F32))]
        found = dot(jnp.concatenate(terms, axis=0), chosen)
        for i, f in enumerate(group):
            part = found[i * 3 * members : (i + 1) * 3 * members]
            total = jnp.where(own_field == float(f), part, total)
    picked[...] = total[:members] + total[members : 2 * members] + total[2 * members :]

    def scatter(step):
        peer = lax.rem(level + step, blocks)
        return pltpu.make_async_remote_copy(
            src_ref=picked.at[pl.ds(pl.multiple_of(peer * share, share), share)],
            dst_ref=parts.at[step],
            send_sem=rs_send.at[step],
            recv_sem=rs_recv.at[step],
            device_id={"blk": peer},
            device_id_type=MESH,
        )

    mine = pl.ds(pl.multiple_of(level * share, share), share)

    def gather(step):
        peer = lax.rem(level + step, blocks)
        return pltpu.make_async_remote_copy(
            src_ref=near.at[0, 1, mine],
            dst_ref=near.at[0, 1, mine],
            send_sem=ag_send.at[step],
            recv_sem=ag_recv.at[step],
            device_id={"blk": peer},
            device_id_type=MESH,
        )

    def gather_arrive(step):
        source = lax.rem(level + blocks - step, blocks)
        at = pl.ds(pl.multiple_of(source * share, share), share)
        pltpu.make_async_remote_copy(
            src_ref=near.at[0, 1, at],
            dst_ref=near.at[0, 1, at],
            send_sem=ag_send.at[step],
            recv_sem=ag_recv.at[step],
            device_id={"blk": source},
            device_id_type=MESH,
        ).wait_recv()

    pl.semaphore_wait(
        barrier, (blocks - 1) + has_left.astype(jnp.int32) + has_right.astype(jnp.int32)
    )
    for step in (4, 3, 5, 2, 6, 1, 7):
        scatter(step).start()
    strips_start(meta, meta_send, meta_recv)

    for step in range(1, blocks):
        scatter(step).wait_recv()
    summed = picked[mine, :]
    for step in range(1, blocks):
        summed = summed + parts[step]
    near[0, 1, mine, :] = summed
    for step in (4, 3, 5, 2, 6, 1, 7):
        gather(step).start()

    def pieces(source):
        at = pl.ds(pl.multiple_of(source * share, share), share)
        right = pltpu.make_async_remote_copy(
            src_ref=near.at[0, 1, at],
            dst_ref=near.at[0, 0, at],
            send_sem=piece_send.at[0, source],
            recv_sem=piece_recv.at[0, source],
            device_id={"tile": jnp.minimum(tile + 1, tiles - 1)},
            device_id_type=MESH,
        )
        left = pltpu.make_async_remote_copy(
            src_ref=near.at[0, 1, at],
            dst_ref=near.at[0, 2, at],
            send_sem=piece_send.at[1, source],
            recv_sem=piece_recv.at[1, source],
            device_id={"tile": jnp.maximum(tile - 1, 0)},
            device_id_type=MESH,
        )
        return right, left

    def piece_start(source):
        right, left = pieces(source)
        pl.when(has_right)(right.start)
        pl.when(has_left)(left.start)

    piece_start(level)

    strips_arrive(meta, meta_send, meta_recv)
    reach_copy.wait()
    reach_here = reach_ref[level].astype(F32) + 1.0
    taper_state[3 * obs :] = jnp.zeros((near_obs - 3 * obs, cells), F32)
    taper_obs[3 * obs :] = jnp.zeros((near_obs - 3 * obs, wide), F32)
    dev_t[3 * obs :] = jnp.zeros((near_obs - 3 * obs, wide), BF16)
    lane_row = lax.broadcasted_iota(jnp.int32, (obs, rows), 1).astype(F32)
    columns = []
    for s in range(3):
        turned = jnp.transpose(
            jnp.concatenate([meta[s], jnp.zeros((LANES - 8, wide), F32)], axis=0)
        )
        columns.append([turned[:obs, i : i + 1] for i in range(3)])
    for s in range(3):
        col, row, lev = columns[s]
        vertical = jnp.maximum(0.0, 1.0 - jnp.abs(level.astype(F32) - lev) / reach_here)
        gap = lane_row - row
        gap = gap * gap
        for c in range(cols):
            across = col - (tile * cols + c).astype(F32)
            close = jnp.maximum(1.0 - (across * across + gap) * (1.0 / (cols * cols)), 0.0)
            taper_state[block(s), c * rows : (c + 1) * rows] = close * close * vertical


    reach_own = jnp.zeros((1, wide), F32)
    for k in range(blocks):
        reach_own = jnp.where(own_level == float(k), reach_ref[k].astype(F32), reach_own)
    reach_own = 1.0 / (reach_own + 1.0)
    for s in range(3):
        col, row, lev = columns[s]
        across = col - own_col
        gap = row - own_row
        close = jnp.maximum(1.0 - (across * across + gap * gap) * (1.0 / (cols * cols)), 0.0)
        vertical = jnp.maximum(0.0, 1.0 - jnp.abs(own_level - lev) * reach_own)
        taper_obs[block(s)] = close * close * vertical

    for step in (1, 7, 2, 6, 3, 5, 4):
        gather_arrive(step)
        piece_start(lax.rem(level + blocks - step, blocks))

    first_half = lax.broadcasted_iota(jnp.int32, (wide, LANES), 1) < members

    def statistics(turn, s):
        prior = near[turn, s]
        average = jnp.sum(prior, axis=0, keepdims=True) * (1.0 / members)
        deviation = prior - average
        flag = meta[s, 4:5, :]
        error = jnp.where(flag > 0, meta[s, 6:7, :], 1.0)
        spread = jnp.sum(deviation * deviation, axis=0, keepdims=True) * (1.0 / (members - 1)) + error
        shrink = 1.0 / (1.0 + jnp.sqrt(error / spread))
        innovation = meta[s, 5:6, :] - average
        coefficient = jnp.where(flag == jnp.asarray(turn + 1, F32), 1.0 / (spread * (members - 1)), 0.0)
        weighted = deviation * coefficient
        turned = jnp.transpose(jnp.concatenate([weighted, weighted], axis=0))
        high = turned.astype(BF16).astype(F32)
        both = jnp.where(first_half, high, turned - high).astype(BF16)[:obs]
        dev_t[block(s)] = jnp.concatenate([both, both], axis=1)
        return innovation - shrink * deviation

    for c in range(cols):
        for f in range(fields):
            state[:, (c * fields + f) * rows : (c * fields + f + 1) * rows] = x_in[
                pl.ds(f * members * cols + c, members, stride=cols), :
            ]
    for source in range(blocks):
        right, left = pieces(source)
        pl.when(has_left)(right.wait_recv)
        pl.when(has_right)(left.wait_recv)

    def batch(turn, carry):
        pulls = [statistics(turn, s)[:, :obs] for s in range(3)]
        factor[...] = side_by_side(pulls, near_obs)
        near[turn + 1, 1] = update(near[turn, 1], dev_t, factor, taper_obs[...])
        strips_start(near.at[turn + 1], halo_send.at[turn + 1], halo_recv.at[turn + 1])
        right_factor[...] = side_by_side(pulls[1:], near_obs - obs)
        for first, last, begin, end, pull in (
            (0, 1, 0, 2 * obs, factor[:, : 2 * obs]),
            (1, cols - 1, 0, near_obs, factor),
            (cols - 1, cols, obs, near_obs, right_factor),
        ):
            at = slice(first * fields * rows, last * fields * rows)
            taper = jnp.concatenate(
                [
                    taper_state[begin:end, c * rows : (c + 1) * rows]
                    for c in range(first, last)
                    for f in range(fields)
                ],
                axis=1,
            )
            state[:, at] = update(state[:, at], dev_t[begin:end], pull, taper)
        strips_arrive(near.at[turn + 1], halo_send.at[turn + 1], halo_recv.at[turn + 1])
        return carry

    lax.fori_loop(0, NBATCH - 1, batch, 0)
    pulls = [statistics(NBATCH - 1, s)[:, :obs] for s in range(3)]
    factor[...] = side_by_side(pulls, near_obs)
    short_factor[...] = side_by_side([pull[:, :SHORT] for pull in pulls], wide)
    counts = [
        jnp.sum(jnp.where(meta[s, 4:5, :] == float(NBATCH), 1.0, 0.0), axis=1, keepdims=True)
        for s in range(3)
    ]
    most[...] = jnp.broadcast_to(functools.reduce(jnp.maximum, counts), (8, LANES))

    strips_sent(meta, meta_send, meta_recv)
    for step in range(1, blocks):
        scatter(step).wait_send()
        gather(step).wait_send()
    for source in range(blocks):
        right, left = pieces(source)
        pl.when(has_right)(right.wait_send)
        pl.when(has_left)(left.wait_send)
    for turn in range(1, NBATCH):
        strips_sent(near.at[turn], halo_send.at[turn], halo_recv.at[turn])


def shards(
    tiles, blocks, ensemble, obs_col, obs_row, obs_level, obs_field, obs_batch, obs_value, obs_error, band_reach
):
    levels, fields, members, cols, rows = ensemble.shape
    obs = obs_col.shape[0]
    wide = 256
    cells = cols * rows
    sizes = (tiles, blocks, fields, members, cols, rows, obs, wide)
    any_space = pl.BlockSpec(memory_space=pltpu.HBM)
    vmem = pl.BlockSpec(memory_space=pltpu.VMEM)
    in_hbm = functools.partial(pltpu.with_memory_space_constraint, memory_space=pltpu.HBM)
    flat = fields * members * cols
    near_obs = -(-3 * obs // 32) * 32
    made = pl.pallas_call(
        functools.partial(kernel, sizes),
        out_shape=(
            jax.ShapeDtypeStruct((members, fields * cells), F32),
            jax.ShapeDtypeStruct((near_obs, wide), BF16),
            jax.ShapeDtypeStruct((2 * members, near_obs), BF16),
            jax.ShapeDtypeStruct((near_obs, cells), F32),
            jax.ShapeDtypeStruct((2 * members, wide), BF16),
            jax.ShapeDtypeStruct((8, LANES), F32),
        ),
        in_specs=[any_space] * 9,
        out_specs=[vmem] * 6,
        scratch_shapes=[
            pltpu.VMEM((flat + 8, rows), F32),
            pltpu.VMEM((NBATCH, 3, members, wide), F32),
            pltpu.VMEM((3, 8, wide), F32),
            pltpu.VMEM((near_obs, wide), F32),
            pltpu.VMEM((members, wide), F32),
            pltpu.VMEM((blocks, members // blocks, wide), F32),
            pltpu.VMEM((2 * members, near_obs - obs), BF16),
            pltpu.VMEM((8, wide), F32),
            pltpu.VMEM((5, 1, obs), jnp.int32),
            pltpu.VMEM((2, 1, obs), F32),
            pltpu.SMEM((blocks,), jnp.int32),
            pltpu.SemaphoreType.DMA,
            pltpu.SemaphoreType.DMA((7,)),
            pltpu.SemaphoreType.DMA((fields,)),
            pltpu.SemaphoreType.DMA((2,)),
            pltpu.SemaphoreType.DMA((2,)),
            pltpu.SemaphoreType.DMA((blocks,)),
            pltpu.SemaphoreType.DMA((blocks,)),
            pltpu.SemaphoreType.DMA((blocks,)),
            pltpu.SemaphoreType.DMA((blocks,)),
            pltpu.SemaphoreType.DMA((NBATCH, 2)),
            pltpu.SemaphoreType.DMA((NBATCH, 2)),
            pltpu.SemaphoreType.DMA((2, blocks)),
            pltpu.SemaphoreType.DMA((2, blocks)),
        ],
        compiler_params=pltpu.CompilerParams(
            collective_id=0, has_side_effects=True, vmem_limit_bytes=VMEM_LIMIT * 2**20
        ),
    )(
        in_hbm(ensemble.reshape(flat, rows)),
        *(
            in_hbm(v.reshape(1, obs))
            for v in (obs_col, obs_row, obs_level, obs_field, obs_batch, obs_value, obs_error)
        ),
        in_hbm(band_reach),
    )
    out = pl.pallas_call(
        functools.partial(finish, (fields, members, cols, rows, obs)),
        out_shape=jax.ShapeDtypeStruct((flat, rows), F32),
        in_specs=[vmem] * 6,
        out_specs=any_space,
        scratch_shapes=[pltpu.VMEM((flat + 8, rows), F32), pltpu.SemaphoreType.DMA((fields,))],
        compiler_params=pltpu.CompilerParams(vmem_limit_bytes=VMEM_LIMIT * 2**20),
    )(*made)
    return out.reshape(levels, fields, members, cols, rows)


def solution(mesh):
    return jax.shard_map(
        functools.partial(shards, mesh.shape["tile"], mesh.shape["blk"]),
        mesh=mesh,
        in_specs=(
            P("blk", None, None, "tile", None),
            P("tile"),
            P("tile"),
            P("tile"),
            P("tile"),
            P("tile"),
            P("tile"),
            P("tile"),
            P(),
        ),
        out_specs=P("blk", None, None, "tile", None),
        check_vma=False,
    )
```
